32 devices in a mesh: au: 4 (over y, x), row: 8 (over z, core).
Axes of the slice: x: 2, y: 2, z: 4, core: 2. Of those that a mesh axis runs over, the one named last changes fastest.
Arguments:
- tokens: bfloat16 [2, 2560, 2048], P(None, ('row', 'au')), may hold values from -6 to 6
- permutation: int32 [2, 2560], replicated, may hold values from 0 to 2559, each once within a row
- lengths: int32 [2, 4], replicated, may hold values from 1 to 2240, 2560 in all within a row
- w_query: bfloat16 [2048, 2048], P(('row', 'au')), may hold values from -0.125 to 0.125
- w_keyval: bfloat16 [2048, 256], P(('row', 'au')), may hold values from -0.125 to 0.125
- w_out: bfloat16 [2048, 2048], P(('row', 'au')), may hold values from -0.75 to 0.75
- w_gate: bfloat16 [2048, 5632], P(('row', 'au')), may hold values from -0.125 to 0.125
- w_up: bfloat16 [2048, 5632], P(('row', 'au')), may hold values from -0.125 to 0.125
- w_down: bfloat16 [5632, 2048], P(('row', 'au')), may hold values from -0.078125 to 0.078125
- attn_gain: bfloat16 [2048], P(('row', 'au')), may hold values from 0.5 to 1.5
- mlp_gain: bfloat16 [2048], P(('row', 'au')), may hold values from 0.5 to 1.5
- out_grad: bfloat16 [2, 2560, 2048], P(None, ('row', 'au')), may hold values from -6 to 6
- kv_partner: bfloat16 [2, 2560, 256], P(None, ('row', 'au')), may hold values from -6 to 6
Outputs:
- result: bfloat16 [2, 2560, 2048], P(None, ('row', 'au'))
- grad_tokens: bfloat16 [2, 2560, 2048], P(None, ('row', 'au'))
- grad_query: float32 [2048, 2048], P(('row', 'au'))
- grad_keyval: float32 [2048, 256], P(('row', 'au'))
- output_weight_gradient: float32 [2048, 2048], P(('row', 'au'))
- grad_gate: float32 [2048, 5632], P(('row', 'au'))
- grad_up: float32 [2048, 5632], P(('row', 'au'))
- grad_down: float32 [5632, 2048], P(('row', 'au'))
- grad_attn_gain: float32 [2048], P(('row', 'au'))
- grad_mlp_gain: float32 [2048], P(('row', 'au'))
The draws below stay inside these ranges and needn't reach their ends.
Inputs may be any that keep to these rules, and one draw needn't show every extreme that they name: `permutation`: each row names every place of its micro-batch once. Each row's 4 lengths sum to 2560; the longest is exactly 2240.
All inputs are finite; a program needn't handle non-finite values.
Results may differ from the reference program's by a relative error of at most 0.019.
Values may be sent and summed in bfloat16 or wider, within the bound.
No kernel may reach another device: no remote copies, remote signals or barrier semaphores. Data moves between devices by JAX's collectives and lax.ppermute only.
A program may use at most 448 MiB of HBM per device.

```python
import math
import jax
import jax.numpy as jnp
import numpy as np
from jax import lax

D = 2048
HQ = 16
HEAD_WIDTH = 128
FF = 5632
MB = 2
NDOC = 4
M = 2560
LMAX = 2240


def strengthened(values, rng, source, target, shards_of, factor):
    def block_of(axis_at):
        return (jnp.arange(values.shape[axis_at]) // (values.shape[axis_at] // shards_of)).reshape((-1,) + (1,) * (values.ndim - 1 - axis_at))

    first = jax.random.permutation(rng, shards_of)[block_of(target)]
    other_side = (block_of(target) + shards_of // 2) % shards_of
    return jnp.where((block_of(source) == first) | (block_of(source) == other_side), factor * values, values)


def level_of(own_key, shape, cuts, smallest, top_value):
    factor_of = 1.0
    for axis_at, parts in cuts:
        draws = jax.random.uniform(jax.random.fold_in(jax.random.fold_in(own_key, 6), axis_at), (parts,), jnp.float32, smallest / len(cuts), top_value / len(cuts))
        factor_of = factor_of * jnp.repeat(jnp.exp(draws), shape[axis_at] // parts).reshape((-1,) + (1,) * (len(shape) - 1 - axis_at))
    return factor_of


def length_profile(amount, total, most, lean):
    loads = [(1 << 20) // math.isqrt(rank ** lean) + 1 for rank in range(2, amount + 1)]
    rest, holding = total - most - (amount - 1), [1] * (amount - 1)
    while rest > 0:
        free = [i for i in range(amount - 1) if holding[i] < most]
        mass, remaining = sum([loads[i] for i in free]), rest
        for i in free:
            extra = min(most - holding[i], max(1, remaining * loads[i] // mass), rest)
            holding[i] = holding[i] + extra
            rest = rest - extra
    return np.array([most] + holding)


def uneven_parts(stream_key, number_of, total, limit, skew):
    if number_of == 2:
        one = jax.random.randint(stream_key, (), max(1, total - limit), min(limit, total - 1) + 1)
        return jnp.stack([one, total - one])
    tallies = jnp.asarray(length_profile(number_of, total, limit, skew), jnp.int32)
    pairs = (number_of - 1) // 2
    source_of, sink = tallies[1:1 + 2 * pairs:2], tallies[2:2 + 2 * pairs:2]
    margin = jnp.minimum(source_of - 1, limit - sink)
    passed = jax.random.randint(jax.random.fold_in(stream_key, 1), (pairs,), 0, 1 << 20) % (margin + 1)
    tallies = tallies.at[1:1 + 2 * pairs:2].set(source_of - passed).at[2:2 + 2 * pairs:2].set(sink + passed)
    return tallies[jax.random.permutation(jax.random.fold_in(stream_key, 2), number_of)]


def gaussian(stream_key, shape, width, limit, split=(), kind=jnp.bfloat16):
    values = jax.random.normal(stream_key, shape, jnp.float32) * width
    if len(split) > 0:
        values = level_of(stream_key, shape, split, -0.22, 0.18) * values
    return jnp.clip(values, min=-limit, max=limit).astype(kind)


def bell_draw_with(own_key, extent, width, limit, shards, heavy, held_as=jnp.bfloat16):
    values = width * jax.random.normal(own_key, extent, jnp.float32)
    if shards:
        values = values * level_of(own_key, extent, shards, -0.22, 0.18)
    return jnp.clip(strengthened(values, jax.random.fold_in(own_key, 3), *heavy), -limit, limit).astype(held_as)


def setup_inputs(seed: int = 0) -> dict:
    streams_of = jax.random.split(jax.random.key(seed), 14)
    return {
        "tokens": bell_draw_with(streams_of[0], (MB, M, D), 1.0, 6.0, ((1, 32),), (1, 2, 32, 2.75)),
        "permutation": jax.vmap(lambda own: jax.random.permutation(own, M))(jax.random.split(streams_of[1], MB)).reshape((MB, M)).astype(jnp.int32),
        "lengths": jax.vmap(lambda own: uneven_parts(own, NDOC, M, LMAX, 2))(jax.random.split(streams_of[2], MB)).reshape((MB, NDOC)).astype(jnp.int32),
        "w_query": gaussian(streams_of[3], (D, HQ * HEAD_WIDTH), D ** -0.5, 0.125, ((0, 32),)),
        "w_keyval": gaussian(streams_of[4], (D, 2 * HEAD_WIDTH), D ** -0.5, 0.125, ((0, 32),)),
        "w_out": gaussian(streams_of[5], (HQ * HEAD_WIDTH, D), (HQ * HEAD_WIDTH // 32) ** -0.5, 0.75, ((0, 32),)),
        "w_gate": gaussian(streams_of[6], (D, FF), D ** -0.5, 0.125, ((0, 32),)),
        "w_up": gaussian(streams_of[7], (D, FF), D ** -0.5, 0.125, ((0, 32),)),
        "w_down": gaussian(streams_of[8], (FF, D), FF ** -0.5, 0.078125, ((0, 32),)),
        "attn_gain": jnp.clip(1.0 + 0.1 * jax.random.normal(streams_of[9], (D,), jnp.float32), 0.5, 1.5).astype(jnp.bfloat16),
        "mlp_gain": jnp.clip(1.0 + 0.1 * jax.random.normal(streams_of[10], (D,), jnp.float32), 0.5, 1.5).astype(jnp.bfloat16),
        "out_grad": gaussian(streams_of[11], (MB, M, D), 1.0, 6.0, ((1, 32),)),
        "kv_partner": gaussian(streams_of[12], (MB, M, 2 * HEAD_WIDTH), 1.0, 6.0, ((1, 32),)),
    }


@jax.custom_vjp
def low(v):
    return lax.optimization_barrier(v.astype(jnp.bfloat16)).astype(jnp.float32)

@jax.custom_vjp
def low_back(v):
    return v

def low_keep(v):
    return (low(v), None)

def low_pass(kept, grad):
    return (grad,)

def back_keep(v):
    return (v, None)

def back_low(kept, grad):
    return (low(grad),)
low.defvjp(low_keep, low_pass)
low_back.defvjp(back_keep, back_low)
norm_eps = 1e-05
theta_base = 10000.0

def exact_dot(left, right):
    return jnp.dot(left, right, precision=lax.Precision.HIGHEST)

def rms_scale(values, gain):
    return values * lax.rsqrt(lax.optimization_barrier(jnp.mean(values * values, axis=-1, keepdims=True)) + norm_eps) * gain

def rotate(values, cosine, sine):
    half = values.shape[-1] // 2
    first = values[..., :half]
    second = values[..., half:]
    return jnp.concatenate([first * cosine - second * sine, second * cosine + first * sine], axis=-1)

def document_info(places, lengths_row):
    starts = (jnp.cumsum(lengths_row) - lengths_row).astype(jnp.int32)
    inside = places[:, None] >= starts[None, :]
    documents = (lax.optimization_barrier(jnp.sum(inside.astype(jnp.int32), axis=1)) - 1).astype(jnp.int32)
    begins = lax.optimization_barrier(jnp.max(jnp.where(inside, starts[None, :], 0), axis=1)).astype(jnp.int32)
    return (documents, places - begins)

def angle_table(positions):
    half = HEAD_WIDTH // 2
    inverse_freq = jnp.exp(-math.log(theta_base) * (2.0 * jnp.arange(half, dtype=jnp.float32) / HEAD_WIDTH))
    angles = positions.astype(jnp.float32)[..., None] * inverse_freq
    return (jnp.cos(angles), jnp.sin(angles))

def attend(query_orig, key_orig, value_orig, documents):
    query_rows = min(512, M)
    key_span = min(M, LMAX + query_rows)
    score_scale = HEAD_WIDTH ** (-0.5)

    def one_block(block_index):
        first_row = (block_index * query_rows).astype(jnp.int32)
        offset = jnp.clip(first_row - LMAX, 0, M - key_span).astype(jnp.int32)
        queries = lax.dynamic_slice_in_dim(query_orig, first_row, query_rows, 0)
        keys = lax.dynamic_slice_in_dim(key_orig, offset, key_span, 0)
        values = lax.dynamic_slice_in_dim(value_orig, offset, key_span, 0)
        query_docs = lax.dynamic_slice_in_dim(documents, first_row, query_rows, 0)
        key_docs = lax.dynamic_slice_in_dim(documents, offset, key_span, 0)
        query_places = first_row + jnp.arange(query_rows, dtype=jnp.int32)
        key_places = offset + jnp.arange(key_span, dtype=jnp.int32)
        visible = (query_docs[:, None] == key_docs[None, :]) & (key_places[None, :] <= query_places[:, None])
        scores = low_back(jnp.einsum('qhd,kd->hqk', queries, keys, precision=lax.Precision.HIGHEST) * score_scale)
        scores = jnp.where(visible[None], scores, -jnp.inf)
        weights = low(jax.nn.softmax(scores, axis=-1))
        return jnp.einsum('hqk,kd->qhd', weights, values, precision=lax.Precision.HIGHEST)
    blocks = lax.map(jax.checkpoint(one_block), jnp.arange(M // query_rows, dtype=jnp.int32))
    return blocks.reshape(M, HQ, HEAD_WIDTH)

def forward_layer(tokens, w_query, w_keyval, w_out, w_gate, w_up, w_down, attn_gain, mlp_gain, permutation, lengths):
    normed = low(rms_scale(tokens, attn_gain))
    query_pre = low_back(exact_dot(normed, w_query)).reshape(MB, M, HQ, HEAD_WIDTH)
    keyval_pre = low_back(exact_dot(normed, w_keyval))
    outputs = []
    shared = []
    for batch_index in range(MB):
        slot_places = permutation[batch_index]
        _, positions = document_info(slot_places, lengths[batch_index])
        cosine, sine = angle_table(positions)
        query = low(low_back(rotate(query_pre[batch_index], cosine[:, None, :], sine[:, None, :])))
        key = low(low_back(rotate(keyval_pre[batch_index, :, :HEAD_WIDTH], cosine, sine)))
        value = low(low_back(keyval_pre[batch_index, :, HEAD_WIDTH:]))
        inverse = jnp.zeros((M,), jnp.int32).at[slot_places].set(jnp.arange(M, dtype=jnp.int32))
        all_docs, _ = document_info(jnp.arange(M, dtype=jnp.int32), lengths[batch_index])
        mixed = attend(query[inverse], key[inverse], value[inverse], all_docs)
        outputs.append(mixed[slot_places])
        shared.append(jnp.concatenate([key, value], axis=-1))
    attended = low(low_back(jnp.stack(outputs).reshape(MB, M, HQ * HEAD_WIDTH)))
    hidden = tokens + low_back(exact_dot(attended, w_out))
    normed_two = low(rms_scale(hidden, mlp_gain))
    gate = low_back(exact_dot(normed_two, w_gate))
    up_part = low_back(exact_dot(normed_two, w_up))
    inner = low(jax.nn.silu(gate) * up_part)
    result = hidden + exact_dot(inner, w_down)
    return (result, jnp.stack(shared))

def reference(tokens, permutation, lengths, w_query, w_keyval, w_out, w_gate, w_up, w_down, attn_gain, mlp_gain, out_grad, kv_partner):
    params = [array.astype(jnp.float32) for array in (tokens, w_query, w_keyval, w_out, w_gate, w_up, w_down, attn_gain, mlp_gain)]

    def bound_layer(*values):
        return forward_layer(*values, permutation, lengths)
    outputs, pullback = jax.vjp(bound_layer, *params)
    grads = pullback((out_grad.astype(jnp.float32), kv_partner.astype(jnp.float32)))
    return (outputs[0].astype(jnp.bfloat16), grads[0].astype(jnp.bfloat16), grads[1], grads[2], grads[3], grads[4], grads[5], grads[6], grads[7], grads[8])
```

```python
import math

import jax
import jax.numpy as jnp
from jax import lax
from jax.sharding import PartitionSpec as P

HQ = 16
HEAD_WIDTH = 128


norm_eps = 1e-05
theta_base = 10000.0


def rotate(values, cosine, sine):
    half = values.shape[-1] // 2
    first = values[..., :half]
    second = values[..., half:]
    return jnp.concatenate(
        [first * cosine - second * sine, second * cosine + first * sine], axis=-1
    )


def rotate_back(grads, cosine, sine):
    half = grads.shape[-1] // 2
    first = grads[..., :half]
    second = grads[..., half:]
    return jnp.concatenate(
        [first * cosine + second * sine, second * cosine - first * sine], axis=-1
    )


def document_info(places, lengths_row):
    starts = jnp.cumsum(lengths_row) - lengths_row
    inside = places[:, None] >= starts[None, :]
    documents = jnp.sum(inside.astype(jnp.int32), axis=1) - 1
    begins = jnp.max(jnp.where(inside, starts[None, :], 0), axis=1)
    return (documents, places - begins)


def angle_table(positions):
    half = HEAD_WIDTH // 2
    inverse_freq = jnp.exp(
        -math.log(theta_base) * (2.0 * jnp.arange(half, dtype=jnp.float32) / HEAD_WIDTH)
    )
    angles = positions.astype(jnp.float32)[..., None] * inverse_freq
    return (jnp.cos(angles), jnp.sin(angles))


def dot32(left, right, dims):
    return lax.dot_general(left, right, (dims, ((), ())), preferred_element_type=jnp.float32)


def spread(values, axis):
    copies = jnp.broadcast_to(values[None], (lax.axis_size(axis),) + values.shape)
    return lax.all_to_all(copies, axis, 0, 0)


def swap(blocks, axis):
    return lax.all_to_all(blocks, axis, 0, 0)


def on_device(
    tokens,
    permutation,
    lengths,
    w_query,
    w_keyval,
    w_out,
    w_gate,
    w_up,
    w_down,
    attn_gain,
    mlp_gain,
    out_grad,
    kv_partner,
):
    low = jnp.bfloat16
    wide = jnp.float32
    batches, local_rows, width = tokens.shape
    across = lax.axis_size("au")
    rows = lax.axis_size("row")
    slot_count = permutation.shape[1]
    q_width = w_query.shape[1]
    kv_width = w_keyval.shape[1]
    own_width = w_query.shape[0]
    ff = w_gate.shape[1]
    ff_here = ff // rows
    q_here = q_width // across
    kv_here = kv_width // across
    group_tokens = across * batches * local_rows
    row_index = lax.axis_index("row")
    au_index = lax.axis_index("au")
    group_first = row_index * across * local_rows
    first_slot = group_first + au_index * local_rows
    score_scale = HEAD_WIDTH ** (-0.5)
    key_rows = min(512, slot_count)
    key_blocks = slot_count // key_rows

    gain_one = attn_gain.astype(wide)[:, None]
    gain_two = mlp_gain.astype(wide)[:, None]
    query_scaled = (w_query.astype(wide) * gain_one).astype(low)
    keyval_scaled = (w_keyval.astype(wide) * gain_one).astype(low)
    gate_scaled = (w_gate.astype(wide) * gain_two).astype(low)
    up_scaled = (w_up.astype(wide) * gain_two).astype(low)

    slot_docs = []
    group_positions = []
    for batch_index in range(batches):
        documents, positions = document_info(permutation[batch_index], lengths[batch_index])
        slot_docs.append(documents)
        group_positions.append(
            lax.dynamic_slice_in_dim(positions, group_first, across * local_rows)
        )
    slot_docs = jnp.stack(slot_docs)
    group_cosine, group_sine = angle_table(jnp.stack(group_positions))
    cosine = lax.dynamic_slice_in_dim(group_cosine, au_index * local_rows, local_rows, 1)
    sine = lax.dynamic_slice_in_dim(group_sine, au_index * local_rows, local_rows, 1)
    group_cosine = group_cosine.reshape(batches, across, local_rows, -1).transpose(1, 0, 2, 3)
    group_sine = group_sine.reshape(batches, across, local_rows, -1).transpose(1, 0, 2, 3)
    query_docs = lax.dynamic_slice_in_dim(slot_docs, first_slot, local_rows, 1)
    query_places = lax.dynamic_slice_in_dim(permutation, first_slot, local_rows, 1)

    def visibility(offset, count):
        key_docs = lax.dynamic_slice_in_dim(slot_docs, offset, count, 1)
        key_places = lax.dynamic_slice_in_dim(permutation, offset, count, 1)
        return (query_docs[:, :, None] == key_docs[:, None, :]) & (
            key_places[:, None, :] <= query_places[:, :, None]
        )

    column_blocks = query_scaled.reshape(own_width, across, q_here).transpose(1, 0, 2)
    keyval_blocks = jnp.broadcast_to(keyval_scaled[None], (across, own_width, kv_width))
    column_blocks = swap(jnp.concatenate([column_blocks, keyval_blocks], axis=-1), "au")
    columns = lax.all_gather(column_blocks, "row", axis=0).reshape(width, q_here + kv_width)

    inputs_wide = tokens.astype(wide)
    inverse_one = lax.rsqrt(jnp.mean(inputs_wide * inputs_wide, axis=-1, keepdims=True) + norm_eps)
    unit_one = inputs_wide * inverse_one
    unit_group = spread(unit_one.astype(low), "au")

    projected = dot32(unit_group, columns, ((3,), (0,)))
    query_group = projected[..., :q_here].reshape(
        across, batches, local_rows, q_here // HEAD_WIDTH, HEAD_WIDTH
    )
    query_group = rotate(query_group, group_cosine[:, :, :, None], group_sine[:, :, :, None])
    query = swap(query_group.astype(low), "au")
    query = query.transpose(1, 2, 0, 3, 4).reshape(batches, local_rows, HQ, HEAD_WIDTH)
    key_group = rotate(
        projected[..., q_here : q_here + HEAD_WIDTH], group_cosine, group_sine
    )
    keyval = jnp.concatenate([key_group, projected[..., q_here + HEAD_WIDTH :]], axis=-1)
    keyval = keyval.astype(low).transpose(1, 0, 2, 3).reshape(batches, -1, kv_width)
    keyval_all = lax.all_gather(keyval, "row", axis=1, tiled=True)

    out_full = lax.all_gather(w_out, ("row", "au"), axis=0, tiled=True)

    ff_blocks = jnp.concatenate(
        [gate_scaled.reshape(own_width, rows, ff_here), up_scaled.reshape(own_width, rows, ff_here)],
        axis=-1,
    ).transpose(1, 0, 2)
    ff_blocks = swap(ff_blocks, "row")
    ff_full = lax.all_gather(ff_blocks, "au", axis=1).reshape(width, 2 * ff_here)
    down_full = lax.all_gather(w_down, "au", axis=0, tiled=True)
    out_grad_rows = lax.all_gather(out_grad, "row", axis=0).reshape(-1, width)

    start_state = (
        jnp.zeros((batches, local_rows, HQ, HEAD_WIDTH), jnp.float32),
        jnp.full((batches, local_rows, HQ), -1e30, jnp.float32),
        jnp.zeros((batches, local_rows, HQ), jnp.float32),
    )

    def absorb(running, block_index):
        weighted, highest, denominator = running
        offset = block_index * key_rows
        incoming_values = lax.dynamic_slice_in_dim(keyval_all, offset, key_rows, 1)
        visible = visibility(offset, key_rows)[:, :, None, :]
        scores = (
            jnp.einsum(
                "azol,atl->azot",
                query,
                incoming_values[..., :HEAD_WIDTH],
                preferred_element_type=jnp.float32,
            )
            * score_scale
        )
        scores = jnp.where(visible, scores, -1e30)
        new_high = jnp.maximum(highest, jnp.max(scores, axis=-1))
        rescale = jnp.exp(highest - new_high)
        weights = jnp.where(visible, jnp.exp(scores - new_high[..., None]), 0.0)
        denominator = denominator * rescale + jnp.sum(weights, axis=-1)
        weighted = weighted * rescale[..., None] + jnp.einsum(
            "cisz,czn->cisn",
            weights.astype(jnp.bfloat16),
            incoming_values[..., HEAD_WIDTH:],
            preferred_element_type=jnp.float32,
        )
        return ((weighted, new_high, denominator), None)

    (weighted, highest, denominator), _ = lax.scan(
        absorb, start_state, jnp.arange(key_blocks, dtype=jnp.int32)
    )
    attended_wide = weighted / denominator[..., None]
    log_mass = highest + jnp.log(denominator)
    attended = attended_wide.astype(low).reshape(batches, local_rows, q_width)
    attended_group = spread(attended, "au")
    hidden = inputs_wide + dot32(attended, out_full, ((2,), (0,)))

    inverse_two = lax.rsqrt(jnp.mean(hidden * hidden, axis=-1, keepdims=True) + norm_eps)
    unit_two = hidden * inverse_two
    unit_rows = lax.all_gather(unit_two.astype(low), "row", axis=0).reshape(-1, width)
    both = dot32(unit_rows, ff_full, ((1,), (0,)))
    gate = both[:, :ff_here]
    up_part = both[:, ff_here:]
    sigmoid_gate = jax.nn.sigmoid(gate)
    inner = (gate * sigmoid_gate * up_part).astype(low)
    grad_inner = dot32(out_grad_rows, down_full, ((1,), (1,)))
    grad_gate = grad_inner * up_part * sigmoid_gate * (1.0 + gate * (1.0 - sigmoid_gate))
    grad_up = grad_inner * gate * sigmoid_gate
    grad_both = jnp.concatenate([grad_gate.astype(low), grad_up.astype(low)], axis=1)
    scaled_two_part = dot32(grad_both, ff_full, ((1,), (1,)))
    scaled_two = lax.psum_scatter(
        scaled_two_part.astype(low).reshape(rows, batches, local_rows, width), "row"
    ).astype(wide)
    result_part = dot32(inner, down_full, ((1,), (0,)))
    result = hidden + lax.psum_scatter(
        result_part.astype(low).reshape(rows, batches, local_rows, width), "row"
    ).astype(wide)

    grad_hidden = out_grad.astype(wide) + inverse_two * (
        scaled_two - unit_two * jnp.mean(scaled_two * unit_two, axis=-1, keepdims=True)
    )
    grad_branch = grad_hidden.astype(low)
    grad_attended = (
        dot32(grad_branch, out_full, ((2,), (1,)))
        .astype(low)
        .reshape(batches, local_rows, HQ, HEAD_WIDTH)
    )
    branch_columns = swap(
        grad_branch.reshape(batches, local_rows, across, -1).transpose(2, 0, 1, 3), "au"
    )

    both_term = dot32(unit_rows, grad_both, ((0,), (0,))).astype(low)
    both_term = both_term.reshape(rows, across, own_width, 2 * ff_here).transpose(1, 0, 2, 3)
    both_term = lax.psum_scatter(
        both_term.reshape(-1, 2 * ff_here), "au", scatter_dimension=0, tiled=True
    )
    both_term = swap(both_term.reshape(rows, own_width, 2 * ff_here), "row").astype(wide)
    gate_term = both_term[..., :ff_here].transpose(1, 0, 2).reshape(own_width, ff)
    up_term = both_term[..., ff_here:].transpose(1, 0, 2).reshape(own_width, ff)
    down_term = dot32(inner, out_grad_rows, ((0,), (0,))).astype(low)
    shard_down = lax.psum_scatter(
        down_term, "au", scatter_dimension=0, tiled=True
    ).astype(wide)
    shard_gain_two = jnp.sum(
        gate_term * w_gate.astype(wide) + up_term * w_up.astype(wide), axis=1
    )
    shard_gate = gate_term * gain_two
    shard_up = up_term * gain_two

    settle = jnp.sum(grad_attended.astype(jnp.float32) * attended_wide, axis=-1)

    def key_block(carried, block_index):
        grad_query_acc, grad_keyval_acc = carried
        first_row = block_index * key_rows
        incoming_values = lax.dynamic_slice_in_dim(keyval_all, first_row, key_rows, 1)
        visible = visibility(first_row, key_rows)[:, :, None, :]
        scores = (
            jnp.einsum(
                "azol,atl->azot",
                query,
                incoming_values[..., :HEAD_WIDTH],
                preferred_element_type=jnp.float32,
            )
            * score_scale
        )
        weights = jnp.where(visible, jnp.exp(scores - log_mass[..., None]), 0.0)
        grad_value = jnp.einsum(
            "fepu,fepc->fuc",
            weights.astype(jnp.bfloat16),
            grad_attended,
            preferred_element_type=jnp.float32,
        )
        grad_weights = jnp.einsum(
            "azol,atl->azot",
            grad_attended,
            incoming_values[..., HEAD_WIDTH:],
            preferred_element_type=jnp.float32,
        )
        score_gradient = (weights * (grad_weights - settle[..., None])).astype(jnp.bfloat16)
        grad_query_acc = (
            grad_query_acc
            + jnp.einsum(
                "cisz,czn->cisn",
                score_gradient,
                incoming_values[..., :HEAD_WIDTH],
                preferred_element_type=jnp.float32,
            )
            * score_scale
        )
        grad_key = (
            jnp.einsum(
                "fepu,fepc->fuc",
                score_gradient,
                query,
                preferred_element_type=jnp.float32,
            )
            * score_scale
        )
        grad_keyval_acc = lax.dynamic_update_slice_in_dim(
            grad_keyval_acc, jnp.concatenate([grad_key, grad_value], axis=-1), first_row, 1
        )
        return ((grad_query_acc, grad_keyval_acc), None)

    start_grads = (
        jnp.zeros((batches, local_rows, HQ, HEAD_WIDTH), jnp.float32),
        jnp.zeros((batches, slot_count, 2 * HEAD_WIDTH), jnp.float32),
    )
    (grad_query_heads, grad_keyval_term), _ = lax.scan(
        key_block, start_grads, jnp.arange(key_blocks, dtype=jnp.int32)
    )
    keyval_blocks = grad_keyval_term.astype(low).reshape(
        batches, rows, across, local_rows, kv_width
    )
    keyval_blocks = swap(keyval_blocks.transpose(2, 1, 0, 3, 4), "au")
    keyval_blocks = jnp.sum(keyval_blocks.astype(wide), axis=0).astype(low)
    grad_keyval_local = jnp.sum(swap(keyval_blocks, "row").astype(wide), axis=0)
    grad_keyval_local = (grad_keyval_local + kv_partner.astype(wide)).astype(low)
    grad_key_pre = rotate_back(grad_keyval_local[..., :HEAD_WIDTH].astype(wide), cosine, sine)
    grad_keyval_pre = jnp.concatenate(
        [grad_key_pre, grad_keyval_local[..., HEAD_WIDTH:].astype(wide)], axis=-1
    ).astype(low)
    grad_query_pre = rotate_back(
        grad_query_heads.astype(low).astype(wide), cosine[:, :, None], sine[:, :, None]
    )
    grad_query_pre = grad_query_pre.astype(low).reshape(batches, local_rows, q_width)

    def column_split(values):
        blocks = values.reshape(batches, local_rows, across, -1).transpose(2, 0, 1, 3)
        return swap(blocks, "au")

    def row_owner(term):
        blocks = term.astype(low).reshape(rows, across, own_width, -1)
        part = lax.psum_scatter(blocks, "row")
        return swap(part, "au").transpose(1, 0, 2).reshape(own_width, -1).astype(wide)

    group_dims = ((0, 1, 2), (0, 1, 2))
    shard_out = row_owner(dot32(attended_group, branch_columns, group_dims))
    query_term = row_owner(dot32(unit_group, column_split(grad_query_pre), group_dims))
    keyval_term = row_owner(dot32(unit_group, column_split(grad_keyval_pre), group_dims))
    shard_gain_one = jnp.sum(query_term * w_query.astype(wide), axis=1) + jnp.sum(
        keyval_term * w_keyval.astype(wide), axis=1
    )
    shard_query = query_term * gain_one
    shard_keyval = keyval_term * gain_one

    query_full = lax.all_gather(query_scaled, ("row", "au"), axis=0, tiled=True)
    keyval_full = columns[:, q_here:]
    scaled_one = dot32(grad_query_pre, query_full, ((2,), (1,))) + dot32(
        grad_keyval_pre, keyval_full, ((2,), (1,))
    )
    grad_inputs = grad_hidden + inverse_one * (
        scaled_one - unit_one * jnp.mean(scaled_one * unit_one, axis=-1, keepdims=True)
    )
    return (
        result.astype(low),
        grad_inputs.astype(low),
        shard_query,
        shard_keyval,
        shard_out,
        shard_gate,
        shard_up,
        shard_down,
        shard_gain_one,
        shard_gain_two,
    )


def solution(mesh):
    return jax.shard_map(
        on_device,
        mesh=mesh,
        in_specs=(
            P(None, ("row", "au"), None),
            P(),
            P(),
            P(("row", "au"), None),
            P(("row", "au"), None),
            P(("row", "au"), None),
            P(("row", "au"), None),
            P(("row", "au"), None),
            P(("row", "au"), None),
            P(("row", "au")),
            P(("row", "au")),
            P(None, ("row", "au"), None),
            P(None, ("row", "au"), None),
        ),
        out_specs=(
            P(None, ("row", "au"), None),
            P(None, ("row", "au"), None),
            P(("row", "au"), None),
            P(("row", "au"), None),
            P(("row", "au"), None),
            P(("row", "au"), None),
            P(("row", "au"), None),
            P(("row", "au"), None),
            P(("row", "au")),
            P(("row", "au")),
        ),
        check_vma=False,
    )
```

```python
import functools
import math

import jax
import jax.numpy as jnp
from jax import lax
from jax.experimental import pallas as pl
from jax.experimental.pallas import tpu as pltpu
from jax.sharding import PartitionSpec as P

HQ = 16
HEAD_WIDTH = 128
LOG2E = math.log2(math.e)


norm_eps = 1e-05
theta_base = 10000.0


def rotate(values, cosine, sine):
    half = values.shape[-1] // 2
    first = values[..., :half]
    second = values[..., half:]
    return jnp.concatenate(
        [first * cosine - second * sine, second * cosine + first * sine], axis=-1
    )


def rotate_back(grads, cosine, sine):
    half = grads.shape[-1] // 2
    first = grads[..., :half]
    second = grads[..., half:]
    return jnp.concatenate(
        [first * cosine + second * sine, second * cosine - first * sine], axis=-1
    )


def document_info(places, lengths_row):
    starts = jnp.cumsum(lengths_row) - lengths_row
    inside = places[:, None] >= starts[None, :]
    documents = jnp.sum(inside.astype(jnp.int32), axis=1) - 1
    begins = jnp.max(jnp.where(inside, starts[None, :], 0), axis=1)
    return (documents, places - begins)


def angle_table(positions):
    half = HEAD_WIDTH // 2
    inverse_freq = jnp.exp(
        -math.log(theta_base) * (2.0 * jnp.arange(half, dtype=jnp.float32) / HEAD_WIDTH)
    )
    angles = positions.astype(jnp.float32)[..., None] * inverse_freq
    return (jnp.cos(angles), jnp.sin(angles))


low = jnp.bfloat16
wide = jnp.float32


def dot32(left, right, dims):
    return lax.dot_general(left, right, (dims, ((), ())), preferred_element_type=jnp.float32)


NN = ((1,), (0,))
NT = ((1,), (1,))
TN = ((0,), (0,))


def head_columns(ref, heads):
    return jnp.concatenate(
        [ref[:, h * HEAD_WIDTH : (h + 1) * HEAD_WIDTH] for h in range(heads)], axis=0
    )


def visible_bias(places, place, start):
    return jnp.where((places <= place) & (places >= start), 0.0, -1e30)


def attend_kernel(heads, q_ref, kv_ref, own_ref, keys_ref, att_ref, wide_ref, mass_ref, bias_ref):
    count = q_ref.shape[0]
    scale = HEAD_WIDTH**-0.5 * LOG2E

    @pl.when(pl.program_id(1) == 0)
    def _():
        bias_ref[...] = visible_bias(keys_ref[...], own_ref[:, 0:1], own_ref[:, 1:2])

    query = head_columns(q_ref, heads)
    keyval = kv_ref[...]
    scores = dot32(query, keyval[:, :HEAD_WIDTH], NT)
    bias = bias_ref[...]
    for h in range(heads):
        part = scores[h * count : (h + 1) * count] * scale + bias
        highest = jnp.max(part, axis=1, keepdims=True)
        weights = jnp.exp2(part - highest)
        mass = jnp.sum(weights, axis=1, keepdims=True)
        attended = dot32(weights.astype(low), keyval[:, HEAD_WIDTH:], NN) / mass
        columns = slice(h * HEAD_WIDTH, (h + 1) * HEAD_WIDTH)
        att_ref[:, columns] = attended.astype(low)
        wide_ref[:, columns] = attended
        mass_ref[:, columns] = jnp.broadcast_to(highest + jnp.log2(mass), (count, HEAD_WIDTH))


def heads_per_step(slots):
    return max(1, min(4, 4 * 2560 // slots))


def attend(query, keyval, own, keys):
    batches, count, width = query.shape
    slots, kv_width = keyval.shape[1:]
    heads = heads_per_step(slots)
    spec = pl.BlockSpec((None, count, heads * HEAD_WIDTH), lambda b, g: (b, 0, g))
    return pl.pallas_call(
        functools.partial(attend_kernel, heads),
        grid=(batches, HQ // heads),
        in_specs=[
            spec,
            pl.BlockSpec((None, slots, kv_width), lambda b, g: (b, 0, 0)),
            pl.BlockSpec((None, count, 2), lambda b, g: (b, 0, 0)),
            pl.BlockSpec((None, 1, slots), lambda b, g: (b, 0, 0)),
        ],
        out_specs=[spec, spec, spec],
        out_shape=[
            jax.ShapeDtypeStruct(query.shape, low),
            jax.ShapeDtypeStruct(query.shape, wide),
            jax.ShapeDtypeStruct(query.shape, wide),
        ],
        scratch_shapes=[pltpu.VMEM((count, slots), wide)],
        cost_estimate=pl.CostEstimate(
            flops=4 * batches * count * width * slots,
            transcendentals=batches * HQ * count * slots,
            bytes_accessed=16 * batches * count * width,
        ),
        compiler_params=pltpu.CompilerParams(vmem_limit_bytes=48 << 20),
    )(query, keyval, own, keys)


def attend_back_kernel(
    heads,
    chunk,
    q_ref,
    g_ref,
    wide_ref,
    mass_ref,
    kv_ref,
    own_ref,
    keys_ref,
    gq_ref,
    gkv_ref,
    bias_ref,
):
    count = q_ref.shape[0]
    slots = keys_ref.shape[0]
    rate = HEAD_WIDTH**-0.5
    scale = rate * LOG2E

    @pl.when(pl.program_id(1) == 0)
    def _():
        bias_ref[...] = visible_bias(keys_ref[...], own_ref[0:1], own_ref[1:2])
        gkv_ref[...] = jnp.zeros_like(gkv_ref)

    query = head_columns(q_ref, heads)
    grads = head_columns(g_ref, heads)
    mass = head_columns(mass_ref, heads)
    settle = jnp.sum(grads.astype(wide) * head_columns(wide_ref, heads), axis=1, keepdims=True)
    lane = lax.broadcasted_iota(jnp.int32, mass.shape, 1)
    stats = jnp.where(lane == 0, mass, settle).T
    mass_row = stats[0:1]
    settle_row = stats[1:2]
    keyval = kv_ref[...]
    grad_query = jnp.zeros((heads * count, HEAD_WIDTH), wide)
    for c in range(slots // chunk):
        span = slice(c * chunk, (c + 1) * chunk)
        key = keyval[span, :HEAD_WIDTH]
        value = keyval[span, HEAD_WIDTH:]
        weights = jnp.exp2(dot32(key, query, NT) * scale + bias_ref[span, :] - mass_row)
        slope = (weights * (dot32(value, grads, NT) - settle_row)).astype(low)
        gkv_ref[span, HEAD_WIDTH:] += dot32(weights.astype(low), grads, NN)
        gkv_ref[span, :HEAD_WIDTH] += dot32(slope, query, NN) * rate
        grad_query = grad_query + dot32(slope, key, TN)
    for h in range(heads):
        gq_ref[:, h * HEAD_WIDTH : (h + 1) * HEAD_WIDTH] = (
            grad_query[h * count : (h + 1) * count] * rate
        ).astype(low)


def attend_back(query, grads, att_wide, mass, keyval, own, keys):
    batches, count, width = query.shape
    slots, kv_width = keyval.shape[1:]
    heads = heads_per_step(slots)
    own = jnp.tile(own, (1, 1, heads))
    spec = pl.BlockSpec((None, count, heads * HEAD_WIDTH), lambda b, g: (b, 0, g))
    kv_spec = pl.BlockSpec((None, slots, kv_width), lambda b, g: (b, 0, 0))
    return pl.pallas_call(
        functools.partial(attend_back_kernel, heads, min(512, slots)),
        grid=(batches, HQ // heads),
        in_specs=[
            spec,
            spec,
            spec,
            spec,
            kv_spec,
            pl.BlockSpec((None, 2, heads * count), lambda b, g: (b, 0, 0)),
            pl.BlockSpec((None, slots, 1), lambda b, g: (b, 0, 0)),
        ],
        out_specs=[spec, kv_spec],
        out_shape=[
            jax.ShapeDtypeStruct(query.shape, low),
            jax.ShapeDtypeStruct(keyval.shape, wide),
        ],
        scratch_shapes=[pltpu.VMEM((slots, heads * count), wide)],
        cost_estimate=pl.CostEstimate(
            flops=10 * batches * count * width * slots,
            transcendentals=batches * HQ * count * slots,
            bytes_accessed=16 * batches * count * width,
        ),
        compiler_params=pltpu.CompilerParams(vmem_limit_bytes=48 << 20),
    )(query, grads, att_wide, mass, keyval, own, keys)


def together(*values):
    return lax.optimization_barrier(values)


def exchange(values, axis, offset):
    members = lax.axis_size(axis)
    return lax.ppermute(values, axis, [(i, i ^ offset) for i in range(members)])


def by_index(parts, place):
    bit = 1
    while bit < len(parts):
        flip = (place & bit) != 0
        parts = [jnp.where(flip, parts[i ^ bit], parts[i]) for i in range(len(parts))]
        bit *= 2
    return parts


def trade_au(parts):
    return [parts[0]] + [exchange(parts[k], "au", k) for k in range(1, len(parts))]


def gather_au(values):
    return trade_au([values] * lax.axis_size("au"))


def core_rows(values):
    core = lax.axis_index("row") % 2
    blocks = values.reshape((values.shape[0] // 2, 2) + values.shape[1:])
    return (
        lax.dynamic_index_in_dim(blocks, core, 1, False),
        lax.dynamic_index_in_dim(blocks, 1 - core, 1, False),
    )


def join_cores(here):
    other = exchange(here, "row", 1)
    first = lax.axis_index("row") % 2 == 0
    pairs = jnp.stack([jnp.where(first, here, other), jnp.where(first, other, here)], axis=1)
    return pairs.reshape((-1,) + here.shape[1:])


def join_rows(parts):
    return join_cores(jnp.stack(by_index(parts, lax.axis_index("row") // 2)))


def reduce_cores(blocks):
    mine, others = core_rows(blocks)
    return mine.astype(wide) + exchange(others.astype(low), "row", 1).astype(wide)


def reduce_chips(here):
    chip = lax.axis_index("row") // 2
    total = lax.dynamic_index_in_dim(here, chip, 0, False)
    here = here.astype(low)
    for k in range(1, here.shape[0]):
        part = lax.dynamic_index_in_dim(here, chip ^ k, 0, False)
        total = total + exchange(part, "row", 2 * k).astype(wide)
    return total


def on_device(
    tokens,
    permutation,
    lengths,
    w_query,
    w_keyval,
    w_out,
    w_gate,
    w_up,
    w_down,
    attn_gain,
    mlp_gain,
    out_grad,
    kv_partner,
):
    batches, local_rows, width = tokens.shape
    across = lax.axis_size("au")
    rows = lax.axis_size("row")
    slot_count = permutation.shape[1]
    q_width = w_query.shape[1]
    kv_width = w_keyval.shape[1]
    own_width = w_query.shape[0]
    ff = w_gate.shape[1]
    ff_here = ff // rows
    ff_own = w_down.shape[0]
    q_here = q_width // across
    row_index = lax.axis_index("row")
    au_index = lax.axis_index("au")
    group_rows = across * local_rows

    gain_one = attn_gain.astype(wide)[:, None]
    gain_two = mlp_gain.astype(wide)[:, None]
    query_scaled = (w_query.astype(wide) * gain_one).astype(low)
    keyval_scaled = (w_keyval.astype(wide) * gain_one).astype(low)
    gate_scaled = (w_gate.astype(wide) * gain_two).astype(low)
    up_scaled = (w_up.astype(wide) * gain_two).astype(low)

    inputs_wide = tokens.astype(wide)
    inverse_one = lax.rsqrt(jnp.mean(inputs_wide * inputs_wide, axis=-1, keepdims=True) + norm_eps)
    unit_one = inputs_wide * inverse_one
    unit_group = jnp.stack(gather_au(unit_one.astype(low)))

    out_rows = lax.all_gather(w_out, "row", axis=0)

    column_blocks = query_scaled.reshape(own_width, across, q_here).transpose(1, 0, 2)
    keyval_blocks = jnp.broadcast_to(keyval_scaled[None], (across, own_width, kv_width))
    column_blocks = lax.all_to_all(
        jnp.concatenate([column_blocks, keyval_blocks], axis=-1), "au", 0, 0
    )
    far_offsets = list(range(2, rows, 2))
    grad_parts = [out_grad] + [exchange(out_grad, "row", k) for k in far_offsets[:-1]]
    column_blocks, unit_group, *grad_parts = together(column_blocks, unit_group, *grad_parts)
    column_rows = lax.all_gather(column_blocks, "row", axis=0)
    columns = column_rows.reshape(width, q_here + kv_width)

    au_order = jnp.arange(across, dtype=jnp.int32) ^ au_index
    places = jnp.take(permutation.reshape(batches, rows, across, local_rows), au_order, axis=2)
    key_places = places.reshape(batches, slot_count)
    group_places = lax.dynamic_index_in_dim(places, row_index, 1, False)
    group_positions = jnp.stack(
        [
            document_info(group_places[b].reshape(-1), lengths[b])[1].reshape(across, local_rows)
            for b in range(batches)
        ],
        axis=1,
    )
    group_cosine, group_sine = angle_table(group_positions)
    own = jnp.stack([group_places[:, 0], group_places[:, 0] - group_positions[0]], axis=1)
    cosine = group_cosine[0]
    sine = group_sine[0]

    ff_blocks = jnp.concatenate(
        [gate_scaled.reshape(own_width, rows, ff_here), up_scaled.reshape(own_width, rows, ff_here)],
        axis=-1,
    ).transpose(1, 0, 2)
    columns, ff_blocks = together(columns, ff_blocks)
    projected = dot32(unit_group, columns, ((3,), (0,)))
    key_group = rotate(projected[..., q_here : q_here + HEAD_WIDTH], group_cosine, group_sine)
    keyval = jnp.concatenate([key_group, projected[..., q_here + HEAD_WIDTH :]], axis=-1)
    keyval = keyval.astype(low).transpose(1, 0, 2, 3).reshape(batches, group_rows, kv_width)
    query_group, keyval = together(projected[..., :q_here], keyval)
    keyval_gate = query_group
    keyval_all = lax.all_gather(keyval, "row", axis=1, tiled=True)
    ff_rows = lax.all_to_all(ff_blocks, "row", 0, 0)
    *out_parts, keyval_gate = together(*gather_au(core_rows(out_rows)[0]), keyval_gate)
    out_half = jnp.stack(by_index(out_parts, au_index), axis=1)
    out_full = join_cores(out_half).reshape(q_width, width)

    query_group = keyval_gate.reshape(
        across, batches, local_rows, q_here // HEAD_WIDTH, HEAD_WIDTH
    )
    query_group = rotate(query_group, group_cosine[:, :, :, None], group_sine[:, :, :, None])
    query_group = query_group.astype(low).reshape(across, batches, local_rows, q_here)
    query = jnp.concatenate(by_index(trade_au(list(query_group)), au_index), axis=-1)

    ff_parts = gather_au(ff_rows)
    grad_parts.append(exchange(grad_parts[0], "row", far_offsets[-1]))
    query, out_full, ff_rows, *grad_parts = together(query, out_full, ff_rows, *grad_parts)
    grad_rows = join_rows(grad_parts).reshape(-1, width)
    attended, att_wide, log_mass = attend(
        query, keyval_all, own.transpose(0, 2, 1), key_places[:, None, :]
    )
    ff_parts[0] = ff_rows
    attended, ff_parts[1], ff_parts[2] = together(attended, ff_parts[1], ff_parts[2])
    attended_kept, *ff_parts = together(attended, *ff_parts)
    ff_full = jnp.zeros((rows, across, own_width, 2 * ff_here), low)
    for k, part in enumerate(ff_parts):
        ff_full = lax.dynamic_update_index_in_dim(ff_full, part, au_index ^ k, 1)
    ff_full = ff_full.reshape(width, 2 * ff_here)
    down_full = jnp.zeros((across, ff_own, width), low)
    for k, part in enumerate(gather_au(w_down)):
        down_full = lax.dynamic_update_index_in_dim(down_full, part, au_index ^ k, 0)
    down_full = down_full.reshape(-1, width)

    hidden = inputs_wide + dot32(attended, out_full, ((2,), (0,)))
    inverse_two = lax.rsqrt(jnp.mean(hidden * hidden, axis=-1, keepdims=True) + norm_eps)
    unit_two = hidden * inverse_two
    unit_rows = lax.all_gather(unit_two.astype(low), "row", axis=0).reshape(-1, width)

    both = dot32(unit_rows, ff_full, NN)
    gate = both[:, :ff_here]
    up_part = both[:, ff_here:]
    sigmoid_gate = jax.nn.sigmoid(gate)
    inner = (gate * sigmoid_gate * up_part).astype(low)
    grad_inner = dot32(grad_rows, down_full, NT)
    grad_gate = grad_inner * up_part * sigmoid_gate * (1.0 + gate * (1.0 - sigmoid_gate))
    grad_up = grad_inner * gate * sigmoid_gate
    grad_both = jnp.concatenate([grad_gate.astype(low), grad_up.astype(low)], axis=1)
    scaled_two = dot32(grad_both, ff_full, NT).astype(low)
    attended_kept, query_columns, unit_rows = together(
        attended_kept, core_rows(column_rows[..., :q_here])[0], unit_rows
    )
    attended_group = jnp.stack(gather_au(attended_kept))
    scaled_two, attended_group = together(scaled_two, attended_group)
    scaled_two = lax.psum_scatter(
        scaled_two.reshape(rows, batches, local_rows, width), "row"
    ).astype(wide)

    both_term = dot32(unit_rows, grad_both, TN).astype(low)
    both_term = both_term.reshape(rows, across, own_width, 2 * ff_here)
    both_parts = [
        lax.dynamic_index_in_dim(both_term, au_index ^ k, 1, False) for k in range(across)
    ]
    both_parts = trade_au(both_parts)
    down_term = dot32(inner, grad_rows, TN).astype(low).reshape(across, ff_own, width)
    down_parts = [
        lax.dynamic_index_in_dim(down_term, au_index ^ k, 0, False) for k in range(across)
    ]
    down_parts = trade_au(down_parts)
    result_part = dot32(inner, down_full, NN).astype(low)
    result_part = result_part.reshape(rows, batches, local_rows, width)
    scaled_two, result_part, down_parts[0], query_columns, *both_parts = together(
        scaled_two, result_part, down_parts[0], query_columns, *both_parts
    )
    query_half = gather_au(query_columns)
    both_term = sum(part.astype(wide) for part in both_parts).astype(low)
    both_term = lax.all_to_all(both_term, "row", 0, 0)
    result_part = lax.psum_scatter(result_part, "row")

    grad_hidden = out_grad.astype(wide) + inverse_two * (
        scaled_two - unit_two * jnp.mean(scaled_two * unit_two, axis=-1, keepdims=True)
    )
    grad_branch = grad_hidden.astype(low)
    grad_att = dot32(grad_branch, out_full, ((2,), (1,))).astype(low)
    query_full = [join_cores(part).reshape(width, q_here) for part in query_half]

    def column_trade(values):
        size = values.shape[-1] // across
        parts = [values[..., i * size : (i + 1) * size] for i in range(across)]
        return jnp.stack(trade_au(by_index(parts, au_index)))

    def owner_columns(part, sizes):
        parts = by_index(trade_au(by_index(list(part), au_index)), au_index)
        ends = [sum(sizes[: i + 1]) for i in range(len(sizes))]
        return [
            jnp.concatenate([p[:, e - n : e] for p in parts], axis=-1).astype(wide)
            for n, e in zip(sizes, ends)
        ]

    group_dims = ((0, 1, 2), (0, 1, 2))
    branch_columns = column_trade(grad_branch)
    out_term = dot32(attended_group, branch_columns, group_dims).astype(low)
    out_term = reduce_chips(reduce_cores(out_term.reshape(rows, across, own_width, -1)))

    grad_query_heads, grad_keyval_term = attend_back(
        query, grad_att, att_wide, log_mass, keyval_all, own, key_places[:, :, None]
    )
    result_part, grad_query_heads, grad_keyval_term = together(
        result_part, grad_query_heads, grad_keyval_term
    )
    result = hidden + result_part.astype(wide)
    blocks = grad_keyval_term.reshape(batches, rows, across, local_rows, kv_width)
    here = reduce_cores(blocks.transpose(1, 0, 2, 3, 4))
    parts = [here[:, :, k] for k in range(across)]
    parts = trade_au([parts[0]] + [part.astype(low) for part in parts[1:]])
    grad_keyval_local = reduce_chips(sum(part.astype(wide) for part in parts))
    grad_keyval_local, out_term = together(grad_keyval_local, out_term)
    grad_keyval_local = (grad_keyval_local + kv_partner.astype(wide)).astype(low)
    grad_key_pre = rotate_back(grad_keyval_local[..., :HEAD_WIDTH].astype(wide), cosine, sine)
    grad_keyval_pre = jnp.concatenate(
        [grad_key_pre, grad_keyval_local[..., HEAD_WIDTH:].astype(wide)], axis=-1
    ).astype(low)
    grad_query_pre = rotate_back(
        grad_query_heads.reshape(batches, local_rows, HQ, HEAD_WIDTH).astype(wide),
        cosine[:, :, None],
        sine[:, :, None],
    )
    grad_query_pre = grad_query_pre.astype(low).reshape(batches, local_rows, q_width)

    query_term = dot32(unit_group, column_trade(grad_query_pre), group_dims).astype(low)
    query_term = lax.psum_scatter(query_term.reshape(rows, across, own_width, -1), "row")
    keyval_term = dot32(unit_group, column_trade(grad_keyval_pre), group_dims)
    keyval_term = reduce_chips(reduce_cores(keyval_term.reshape(rows, across, own_width, -1)))
    query_term, both_term = together(query_term, both_term)
    both_term = both_term.astype(wide)
    shard_out, query_term, keyval_term = owner_columns(
        jnp.concatenate([out_term.astype(low), query_term, keyval_term.astype(low)], axis=-1),
        [q_here, q_here, kv_width // across],
    )

    gate_term = both_term[..., :ff_here].transpose(1, 0, 2).reshape(own_width, ff)
    up_term = both_term[..., ff_here:].transpose(1, 0, 2).reshape(own_width, ff)
    shard_gain_two = jnp.sum(
        gate_term * w_gate.astype(wide) + up_term * w_up.astype(wide), axis=1
    )
    shard_gate = gate_term * gain_two
    shard_up = up_term * gain_two
    shard_down = sum(part.astype(wide) for part in down_parts)
    shard_gain_one = jnp.sum(query_term * w_query.astype(wide), axis=1) + jnp.sum(
        keyval_term * w_keyval.astype(wide), axis=1
    )
    shard_query = query_term * gain_one
    shard_keyval = keyval_term * gain_one

    scaled_one = dot32(grad_keyval_pre, columns[:, q_here:], ((2,), (1,)))
    grad_query_parts = by_index(
        [grad_query_pre[..., i * q_here : (i + 1) * q_here] for i in range(across)], au_index
    )
    for part, weight in zip(grad_query_parts, query_full):
        scaled_one = scaled_one + dot32(part, weight, ((2,), (1,)))
    grad_inputs = grad_hidden + inverse_one * (
        scaled_one - unit_one * jnp.mean(scaled_one * unit_one, axis=-1, keepdims=True)
    )
    return (
        result.astype(low),
        grad_inputs.astype(low),
        shard_query,
        shard_keyval,
        shard_out,
        shard_gate,
        shard_up,
        shard_down,
        shard_gain_one,
        shard_gain_two,
    )


def solution(mesh):
    return jax.shard_map(
        on_device,
        mesh=mesh,
        in_specs=(
            P(None, ("row", "au"), None),
            P(),
            P(),
            P(("row", "au"), None),
            P(("row", "au"), None),
            P(("row", "au"), None),
            P(("row", "au"), None),
            P(("row", "au"), None),
            P(("row", "au"), None),
            P(("row", "au")),
            P(("row", "au")),
            P(None, ("row", "au"), None),
            P(None, ("row", "au"), None),
        ),
        out_specs=(
            P(None, ("row", "au"), None),
            P(None, ("row", "au"), None),
            P(("row", "au"), None),
            P(("row", "au"), None),
            P(("row", "au"), None),
            P(("row", "au"), None),
            P(("row", "au"), None),
            P(("row", "au"), None),
            P(("row", "au")),
            P(("row", "au")),
        ),
        check_vma=False,
    )
```

```python
import functools
import math

import jax
import jax.numpy as jnp
from jax import lax
from jax.experimental import pallas as pl
from jax.experimental.pallas import tpu as pltpu
from jax.sharding import PartitionSpec as P

HQ = 16
HEAD_WIDTH = 128
LOG2E = math.log2(math.e)


norm_eps = 1e-05
theta_base = 10000.0


def rotate(values, cosine, sine):
    half = values.shape[-1] // 2
    first = values[..., :half]
    second = values[..., half:]
    return jnp.concatenate(
        [first * cosine - second * sine, second * cosine + first * sine], axis=-1
    )


def rotate_back(grads, cosine, sine):
    half = grads.shape[-1] // 2
    first = grads[..., :half]
    second = grads[..., half:]
    return jnp.concatenate(
        [first * cosine + second * sine, second * cosine - first * sine], axis=-1
    )


def document_info(places, lengths_row):
    starts = jnp.cumsum(lengths_row) - lengths_row
    inside = places[:, None] >= starts[None, :]
    documents = jnp.sum(inside.astype(jnp.int32), axis=1) - 1
    begins = jnp.max(jnp.where(inside, starts[None, :], 0), axis=1)
    return (documents, places - begins)


def angle_table(positions):
    half = HEAD_WIDTH // 2
    inverse_freq = jnp.exp(
        -math.log(theta_base) * (2.0 * jnp.arange(half, dtype=jnp.float32) / HEAD_WIDTH)
    )
    angles = positions.astype(jnp.float32)[..., None] * inverse_freq
    return (jnp.cos(angles), jnp.sin(angles))


low = jnp.bfloat16
wide = jnp.float32


def dot32(left, right, dims):
    return lax.dot_general(left, right, (dims, ((), ())), preferred_element_type=jnp.float32)


NN = ((1,), (0,))
NT = ((1,), (1,))
TN = ((0,), (0,))


def head_columns(ref, heads):
    return jnp.concatenate(
        [ref[:, h * HEAD_WIDTH : (h + 1) * HEAD_WIDTH] for h in range(heads)], axis=0
    )


def visible_bias(places, place, start):
    return jnp.where((places <= place) & (places >= start), 0.0, -1e30)


def attend_kernel(heads, q_ref, kv_ref, own_ref, keys_ref, att_ref, wide_ref, mass_ref, bias_ref):
    count = q_ref.shape[0]
    scale = HEAD_WIDTH**-0.5 * LOG2E

    @pl.when(pl.program_id(1) == 0)
    def _():
        bias_ref[...] = visible_bias(keys_ref[...], own_ref[:, 0:1], own_ref[:, 1:2])

    query = head_columns(q_ref, heads)
    keyval = kv_ref[...]
    scores = dot32(query, keyval[:, :HEAD_WIDTH], NT)
    bias = bias_ref[...]
    for h in range(heads):
        part = scores[h * count : (h + 1) * count] * scale + bias
        highest = jnp.max(part, axis=1, keepdims=True)
        weights = jnp.exp2(part - highest)
        mass = jnp.sum(weights, axis=1, keepdims=True)
        attended = dot32(weights.astype(low), keyval[:, HEAD_WIDTH:], NN) / mass
        columns = slice(h * HEAD_WIDTH, (h + 1) * HEAD_WIDTH)
        att_ref[:, columns] = attended.astype(low)
        wide_ref[:, columns] = attended
        mass_ref[:, columns] = jnp.broadcast_to(highest + jnp.log2(mass), (count, HEAD_WIDTH))


def heads_per_step(slots):
    return max(1, min(4, 4 * 2560 // slots))


def attend(query, keyval, own, keys):
    batches, count, width = query.shape
    slots, kv_width = keyval.shape[1:]
    heads = heads_per_step(slots)
    spec = pl.BlockSpec((None, count, heads * HEAD_WIDTH), lambda b, g: (b, 0, g))
    return pl.pallas_call(
        functools.partial(attend_kernel, heads),
        grid=(batches, HQ // heads),
        in_specs=[
            spec,
            pl.BlockSpec((None, slots, kv_width), lambda b, g: (b, 0, 0)),
            pl.BlockSpec((None, count, 2), lambda b, g: (b, 0, 0)),
            pl.BlockSpec((None, 1, slots), lambda b, g: (b, 0, 0)),
        ],
        out_specs=[spec, spec, spec],
        out_shape=[
            jax.ShapeDtypeStruct(query.shape, low),
            jax.ShapeDtypeStruct(query.shape, wide),
            jax.ShapeDtypeStruct(query.shape, wide),
        ],
        scratch_shapes=[pltpu.VMEM((count, slots), wide)],
        cost_estimate=pl.CostEstimate(
            flops=4 * batches * count * width * slots,
            transcendentals=batches * HQ * count * slots,
            bytes_accessed=16 * batches * count * width,
        ),
        compiler_params=pltpu.CompilerParams(vmem_limit_bytes=48 << 20),
    )(query, keyval, own, keys)


def attend_back_kernel(
    heads,
    chunk,
    q_ref,
    g_ref,
    wide_ref,
    mass_ref,
    kv_ref,
    own_ref,
    keys_ref,
    gq_ref,
    gkv_ref,
    bias_ref,
):
    count = q_ref.shape[0]
    slots = keys_ref.shape[0]
    rate = HEAD_WIDTH**-0.5
    scale = rate * LOG2E

    @pl.when(pl.program_id(1) == 0)
    def _():
        bias_ref[...] = visible_bias(keys_ref[...], own_ref[0:1], own_ref[1:2])
        gkv_ref[...] = jnp.zeros_like(gkv_ref)

    query = head_columns(q_ref, heads)
    grads = head_columns(g_ref, heads)
    mass = head_columns(mass_ref, heads)
    settle = jnp.sum(grads.astype(wide) * head_columns(wide_ref, heads), axis=1, keepdims=True)
    lane = lax.broadcasted_iota(jnp.int32, mass.shape, 1)
    stats = jnp.where(lane == 0, mass, settle).T
    mass_row = stats[0:1]
    settle_row = stats[1:2]
    keyval = kv_ref[...]
    grad_query = jnp.zeros((heads * count, HEAD_WIDTH), wide)
    for c in range(slots // chunk):
        span = slice(c * chunk, (c + 1) * chunk)
        key = keyval[span, :HEAD_WIDTH]
        value = keyval[span, HEAD_WIDTH:]
        weights = jnp.exp2(dot32(key, query, NT) * scale + bias_ref[span, :] - mass_row)
        slope = (weights * (dot32(value, grads, NT) - settle_row)).astype(low)
        gkv_ref[span, HEAD_WIDTH:] += dot32(weights.astype(low), grads, NN)
        gkv_ref[span, :HEAD_WIDTH] += dot32(slope, query, NN) * rate
        grad_query = grad_query + dot32(slope, key, TN)
    for h in range(heads):
        gq_ref[:, h * HEAD_WIDTH : (h + 1) * HEAD_WIDTH] = (
            grad_query[h * count : (h + 1) * count] * rate
        ).astype(low)


def attend_back(query, grads, att_wide, mass, keyval, own, keys, batch):
    batches, count, width = query.shape
    slots, kv_width = keyval.shape[1:]
    heads = heads_per_step(slots)
    own = jnp.tile(own, (1, 1, heads))
    spec = pl.BlockSpec((None, count, heads * HEAD_WIDTH), lambda b, g: (batch, 0, g))
    return pl.pallas_call(
        functools.partial(attend_back_kernel, heads, min(512, slots)),
        grid=(1, HQ // heads),
        in_specs=[
            spec,
            spec,
            spec,
            spec,
            pl.BlockSpec((None, slots, kv_width), lambda b, g: (batch, 0, 0)),
            pl.BlockSpec((None, 2, heads * count), lambda b, g: (batch, 0, 0)),
            pl.BlockSpec((None, slots, 1), lambda b, g: (batch, 0, 0)),
        ],
        out_specs=[
            pl.BlockSpec((None, count, heads * HEAD_WIDTH), lambda b, g: (b, 0, g)),
            pl.BlockSpec((None, slots, kv_width), lambda b, g: (b, 0, 0)),
        ],
        out_shape=[
            jax.ShapeDtypeStruct((1, count, width), low),
            jax.ShapeDtypeStruct((1, slots, kv_width), wide),
        ],
        scratch_shapes=[pltpu.VMEM((slots, heads * count), wide)],
        cost_estimate=pl.CostEstimate(
            flops=10 * count * width * slots,
            transcendentals=HQ * count * slots,
            bytes_accessed=16 * count * width,
        ),
        compiler_params=pltpu.CompilerParams(vmem_limit_bytes=48 << 20),
    )(query, grads, att_wide, mass, keyval, own, keys)


def together(*values):
    return lax.optimization_barrier(values)


def exchange(values, axis, offset):
    members = lax.axis_size(axis)
    return lax.ppermute(values, axis, [(i, i ^ offset) for i in range(members)])


def by_index(parts, place):
    bit = 1
    while bit < len(parts):
        flip = (place & bit) != 0
        parts = [jnp.where(flip, parts[i ^ bit], parts[i]) for i in range(len(parts))]
        bit *= 2
    return parts


def trade_au(parts):
    return [parts[0]] + [exchange(parts[k], "au", k) for k in range(1, len(parts))]


def gather_au(values):
    return trade_au([values] * lax.axis_size("au"))


def bits_of(members):
    return [1 << i for i in range(members.bit_length() - 1)]


def reduce_send(held, bit):
    keys = [k for k in sorted(held) if k & bit]
    return exchange(jnp.stack([held[k] for k in keys]).astype(low), "au", bit)


def reduce_add(held, bit, got):
    keys = [k for k in sorted(held) if k & bit]
    return {
        k ^ bit: held[k ^ bit].astype(wide) + got[i].astype(wide) for i, k in enumerate(keys)
    }


def reduce_au_first(lists):
    bits = bits_of(lax.axis_size("au"))
    return [reduce_send(dict(enumerate(lists[i])), bits[i % len(bits)]) for i in range(2)]


def reduce_au_rest(lists, got):
    bits = bits_of(lax.axis_size("au"))
    done = []
    for i in range(2):
        held = reduce_add(dict(enumerate(lists[i])), bits[i % len(bits)], got[i])
        for j in range(1, len(bits)):
            bit = bits[(i + j) % len(bits)]
            held = reduce_add(held, bit, reduce_send(held, bit))
        done.append(held[0])
    return done


def core_rows(values):
    core = lax.axis_index("row") % 2
    blocks = values.reshape((values.shape[0] // 2, 2) + values.shape[1:])
    return (
        lax.dynamic_index_in_dim(blocks, core, 1, False),
        lax.dynamic_index_in_dim(blocks, 1 - core, 1, False),
    )


def by_core(values):
    rows = lax.axis_size("row")
    blocks = values.reshape(values.shape[:-1] + (rows // 2, 2, values.shape[-1] // rows))
    first = lax.axis_index("row") % 2 == 0
    low_rows, high_rows = blocks[..., 0, :], blocks[..., 1, :]
    flat = values.shape[:-1] + (values.shape[-1] // 2,)
    return (
        jnp.where(first, low_rows, high_rows).reshape(flat),
        jnp.where(first, high_rows, low_rows).reshape(flat),
    )


def reduce_cores(blocks):
    mine, others = core_rows(blocks)
    return mine.astype(wide) + exchange(others.astype(low), "row", 1).astype(wide)


def reduce_chips(here):
    chip = lax.axis_index("row") // 2
    total = lax.dynamic_index_in_dim(here, chip, 0, False)
    here = here.astype(low)
    for k in range(1, here.shape[0]):
        part = lax.dynamic_index_in_dim(here, chip ^ k, 0, False)
        total = total + exchange(part, "row", 2 * k).astype(wide)
    return total


def on_device(
    tokens,
    permutation,
    lengths,
    w_query,
    w_keyval,
    w_out,
    w_gate,
    w_up,
    w_down,
    attn_gain,
    mlp_gain,
    out_grad,
    kv_partner,
):
    batches, local_rows, width = tokens.shape
    across = lax.axis_size("au")
    rows = lax.axis_size("row")
    slot_count = permutation.shape[1]
    q_width = w_query.shape[1]
    kv_width = w_keyval.shape[1]
    own_width = w_query.shape[0]
    ff = w_gate.shape[1]
    ff_here = ff // rows
    ff_own = w_down.shape[0]
    q_here = q_width // across
    row_index = lax.axis_index("row")
    au_index = lax.axis_index("au")
    group_rows = across * local_rows

    gain_one = attn_gain.astype(wide)[:, None]
    gain_two = mlp_gain.astype(wide)[:, None]
    query_scaled = (w_query.astype(wide) * gain_one).astype(low)
    keyval_scaled = (w_keyval.astype(wide) * gain_one).astype(low)
    gate_scaled = (w_gate.astype(wide) * gain_two).astype(low)
    up_scaled = (w_up.astype(wide) * gain_two).astype(low)

    inputs_wide = tokens.astype(wide)
    inverse_one = lax.rsqrt(jnp.mean(inputs_wide * inputs_wide, axis=-1, keepdims=True) + norm_eps)
    unit_one = inputs_wide * inverse_one
    unit_group = jnp.stack(gather_au(unit_one.astype(low)))

    out_rows = lax.all_gather(w_out, "row", axis=0)

    column_blocks = query_scaled.reshape(own_width, across, q_here).transpose(1, 0, 2)
    keyval_blocks = jnp.broadcast_to(keyval_scaled[None], (across, own_width, kv_width))
    column_blocks = lax.all_to_all(
        jnp.concatenate([column_blocks, keyval_blocks], axis=-1), "au", 0, 0
    )
    ff_blocks = jnp.concatenate(
        [gate_scaled.reshape(own_width, rows, ff_here), up_scaled.reshape(own_width, rows, ff_here)],
        axis=-1,
    ).transpose(1, 0, 2)
    column_blocks, unit_group, out_rows, ff_blocks = together(
        column_blocks, unit_group, out_rows, ff_blocks
    )
    column_rows = lax.all_gather(column_blocks, "row", axis=0)
    columns = column_rows.reshape(width, q_here + kv_width)

    au_order = jnp.arange(across, dtype=jnp.int32) ^ au_index
    places = jnp.take(permutation.reshape(batches, rows, across, local_rows), au_order, axis=2)
    key_places = places.reshape(batches, slot_count)
    group_places = lax.dynamic_index_in_dim(places, row_index, 1, False)
    group_positions = jnp.stack(
        [
            document_info(group_places[b].reshape(-1), lengths[b])[1].reshape(across, local_rows)
            for b in range(batches)
        ],
        axis=1,
    )
    group_cosine, group_sine = angle_table(group_positions)
    own = jnp.stack([group_places[:, 0], group_places[:, 0] - group_positions[0]], axis=1)
    cosine = group_cosine[0]
    sine = group_sine[0]

    out_parts = gather_au(core_rows(out_rows)[0])
    columns, ff_blocks, out_parts[1] = together(columns, ff_blocks, out_parts[1])
    ff_rows = lax.all_to_all(ff_blocks, "row", 0, 0)
    projected = dot32(unit_group, columns, ((3,), (0,)))
    key_group = rotate(projected[..., q_here : q_here + HEAD_WIDTH], group_cosine, group_sine)
    keyval = jnp.concatenate([key_group, projected[..., q_here + HEAD_WIDTH :]], axis=-1)
    keyval = keyval.astype(low).transpose(1, 0, 2, 3).reshape(batches, group_rows, kv_width)
    query_group, keyval, w_down, *out_parts = together(
        projected[..., :q_here], keyval, w_down, *out_parts
    )
    down_parts = gather_au(w_down)
    keyval_all = lax.all_gather(keyval, "row", axis=1, tiled=True)
    query_group = query_group.reshape(
        across, batches, local_rows, q_here // HEAD_WIDTH, HEAD_WIDTH
    )
    query_group = rotate(query_group, group_cosine[:, :, :, None], group_sine[:, :, :, None])
    query_group = query_group.astype(low).reshape(across, batches, local_rows, q_here)
    query = jnp.concatenate(by_index(trade_au(list(query_group)), au_index), axis=-1)

    out_half = jnp.zeros((rows // 2, across, own_width, width), low)
    for k, part in enumerate(out_parts):
        out_half = lax.dynamic_update_index_in_dim(out_half, part, au_index ^ k, 1)
    out_half = out_half.reshape(-1, width)
    out_other = exchange(out_half, "row", 1)

    down_full = jnp.zeros((across, ff_own, width), low)
    for k, part in enumerate(down_parts):
        down_full = lax.dynamic_update_index_in_dim(down_full, part, au_index ^ k, 0)
    down_full = down_full.reshape(-1, width)

    key_columns = key_places[:, :, None]
    (
        grads_own,
        keyval_all,
        ff_rows,
        query,
        out_other,
        down_full,
        key_columns,
    ) = together(out_grad, keyval_all, ff_rows, query, out_other, down_full, key_columns)
    grad_rows = lax.all_gather(grads_own, "row", axis=0).reshape(-1, width)
    ff_parts = gather_au(ff_rows)
    attended, att_wide, log_mass = attend(
        query, keyval_all, own.transpose(0, 2, 1), key_places[:, None, :]
    )
    ff_parts[0] = ff_rows
    attended, ff_parts[1], ff_parts[2] = together(attended, ff_parts[1], ff_parts[2])
    attended_kept = attended
    ff_full = jnp.zeros((rows, across, own_width, 2 * ff_here), low)
    for k, part in enumerate(ff_parts):
        ff_full = lax.dynamic_update_index_in_dim(ff_full, part, au_index ^ k, 1)
    ff_full = ff_full.reshape(width, 2 * ff_here)
    attended_mine, attended_other = by_core(attended)
    hidden = inputs_wide + (
        dot32(attended_mine, out_half, ((2,), (0,))) + dot32(attended_other, out_other, ((2,), (0,)))
    )
    inverse_two = lax.rsqrt(jnp.mean(hidden * hidden, axis=-1, keepdims=True) + norm_eps)
    unit_two = hidden * inverse_two
    unit_low, attended_kept, query_columns = together(
        unit_two.astype(low), attended_kept, core_rows(column_rows[..., :q_here])[0]
    )
    unit_low, grad_rows = together(unit_low, grad_rows)
    unit_rows = lax.all_gather(unit_low, "row", axis=0).reshape(-1, width)
    attended_group = jnp.stack(gather_au(attended_kept))
    query_half = gather_au(query_columns)
    pair = lax.dynamic_update_index_in_dim(
        jnp.zeros((rows // 2, 2) + (across * own_width, width), low),
        out_half.reshape(rows // 2, -1, width),
        row_index % 2,
        1,
    )
    out_full = lax.dynamic_update_index_in_dim(
        pair, out_other.reshape(rows // 2, -1, width), 1 - row_index % 2, 1
    ).reshape(q_width, width)
    unit_rows, out_full = together(unit_rows, out_full)

    both = dot32(unit_rows, ff_full, NN)
    gate = both[:, :ff_here]
    up_part = both[:, ff_here:]
    sigmoid_gate = jax.nn.sigmoid(gate)
    inner = (gate * sigmoid_gate * up_part).astype(low)
    grad_inner = dot32(grad_rows, down_full, NT)
    grad_gate = grad_inner * up_part * sigmoid_gate * (1.0 + gate * (1.0 - sigmoid_gate))
    grad_up = grad_inner * gate * sigmoid_gate
    grad_both = jnp.concatenate([grad_gate.astype(low), grad_up.astype(low)], axis=1)
    scaled_two = dot32(grad_both, ff_full, NT).astype(low)
    scaled_two, attended_group, *query_half = together(scaled_two, attended_group, *query_half)
    scaled_two = lax.psum_scatter(
        scaled_two.reshape(rows, batches, local_rows, width), "row"
    ).astype(wide)

    both_term = dot32(unit_rows, grad_both, TN).astype(low)
    both_term = both_term.reshape(rows, across, own_width, 2 * ff_here)
    both_parts = [
        lax.dynamic_index_in_dim(both_term, au_index ^ k, 1, False) for k in range(across)
    ]
    half_rows = own_width // 2
    both_lists = [
        [part[:, i * half_rows : (i + 1) * half_rows] for part in both_parts] for i in range(2)
    ]
    both_first = reduce_au_first(both_lists)
    down_term = dot32(inner, grad_rows, TN).astype(low).reshape(across, ff_own, width)
    down_parts = [
        lax.dynamic_index_in_dim(down_term, au_index ^ k, 0, False) for k in range(across)
    ]
    result_part = dot32(inner, down_full, NN).astype(low)
    result_part = result_part.reshape(rows, batches, local_rows, width)
    query_half = jnp.stack(query_half).reshape(across, rows // 2, -1, q_here)
    query_other = exchange(query_half, "row", 1)
    pair = lax.dynamic_update_index_in_dim(
        jnp.zeros((across, rows // 2, 2) + query_half.shape[2:], low), query_half, row_index % 2, 2
    )
    query_full = lax.dynamic_update_index_in_dim(pair, query_other, 1 - row_index % 2, 2)
    query_full = query_full.reshape(across, width, q_here)
    scaled_two, result_part, down_parts, both_first, query_full = together(
        scaled_two, result_part, down_parts, both_first, query_full
    )
    both_term = jnp.concatenate(reduce_au_rest(both_lists, both_first), axis=1).astype(low)
    down_parts = trade_au(down_parts)
    result_part = lax.psum_scatter(result_part, "row")

    grad_hidden = out_grad.astype(wide) + inverse_two * (
        scaled_two - unit_two * jnp.mean(scaled_two * unit_two, axis=-1, keepdims=True)
    )
    grad_branch = grad_hidden.astype(low)
    grad_att = dot32(grad_branch, out_full, ((2,), (1,))).astype(low)

    def column_trade(values):
        size = values.shape[-1] // across
        parts = [values[..., i * size : (i + 1) * size] for i in range(across)]
        return jnp.stack(trade_au(by_index(parts, au_index)))

    def owner_columns(part, sizes):
        parts = by_index(trade_au(by_index(list(part), au_index)), au_index)
        ends = [sum(sizes[: i + 1]) for i in range(len(sizes))]
        return [
            jnp.concatenate([p[:, e - n : e] for p in parts], axis=-1).astype(wide)
            for n, e in zip(sizes, ends)
        ]

    group_dims = ((0, 1, 2), (0, 1, 2))
    branch_columns = column_trade(grad_branch)
    grad_query_heads = []
    grad_keyval_term = []
    for b in range(batches):
        grad_query_b, grad_keyval_b = attend_back(
            query, grad_att, att_wide, log_mass, keyval_all, own, key_columns, b
        )
        blocks = grad_keyval_b.reshape(rows, across, local_rows, kv_width)
        mine, others = core_rows(blocks)
        others = exchange(others.astype(low), "row", 1)
        if b == 0:
            grad_query_b, branch_columns, grad_att, both_term = together(
                grad_query_b, branch_columns, grad_att, both_term
            )
            both_term = lax.all_to_all(both_term, "row", 0, 0)
            out_term = dot32(attended_group, branch_columns, group_dims).astype(low)
            grad_att, out_term = together(grad_att, out_term)
            out_term = lax.psum_scatter(out_term.reshape(rows, across, own_width, -1), "row")
        grad_query_heads.append(grad_query_b)
        grad_keyval_term.append(mine + others.astype(wide))
    grad_query_heads = jnp.concatenate(grad_query_heads)
    here = jnp.stack(grad_keyval_term, axis=1)
    grad_query_heads, down_parts[1] = together(grad_query_heads, down_parts[1])

    grad_query_pre = rotate_back(
        grad_query_heads.reshape(batches, local_rows, HQ, HEAD_WIDTH).astype(wide),
        cosine[:, :, None],
        sine[:, :, None],
    )
    grad_query_pre = grad_query_pre.astype(low).reshape(batches, local_rows, q_width)
    query_term = dot32(unit_group, column_trade(grad_query_pre), group_dims).astype(low)
    query_term, result_part = together(query_term, result_part)
    result = hidden + result_part.astype(wide)

    parts = [here[:, :, k] for k in range(across)]
    parts = trade_au([parts[0]] + [part.astype(low) for part in parts[1:]])
    grad_keyval_local = reduce_chips(sum(part.astype(wide) for part in parts))
    grad_keyval_local, both_term = together(grad_keyval_local, both_term)
    grad_keyval_local = (grad_keyval_local + kv_partner.astype(wide)).astype(low)
    grad_key_pre = rotate_back(grad_keyval_local[..., :HEAD_WIDTH].astype(wide), cosine, sine)
    grad_keyval_pre = jnp.concatenate(
        [grad_key_pre, grad_keyval_local[..., HEAD_WIDTH:].astype(wide)], axis=-1
    ).astype(low)
    query_term = lax.psum_scatter(query_term.reshape(rows, across, own_width, -1), "row")
    keyval_term = dot32(unit_one.astype(low), grad_keyval_pre, ((0, 1), (0, 1))).astype(low)
    keyval_term = keyval_term.reshape(rows, across, own_width, kv_width)
    parts = [
        lax.dynamic_index_in_dim(keyval_term, au_index ^ k, 1, False) for k in range(across)
    ]
    keyval_term = sum(part.astype(wide) for part in trade_au(parts))
    keyval_term = reduce_chips(reduce_cores(keyval_term))
    both_term = both_term.astype(wide)
    shard_out, query_term = owner_columns(
        jnp.concatenate([out_term, query_term], axis=-1), [q_here, q_here]
    )

    gate_term = both_term[..., :ff_here].transpose(1, 0, 2).reshape(own_width, ff)
    up_term = both_term[..., ff_here:].transpose(1, 0, 2).reshape(own_width, ff)
    shard_down = sum(part.astype(wide) for part in down_parts)
    shard_gain_two = jnp.sum(
        gate_term * w_gate.astype(wide) + up_term * w_up.astype(wide), axis=1
    )
    shard_gate = gate_term * gain_two
    shard_up = up_term * gain_two
    shard_gain_one = jnp.sum(query_term * w_query.astype(wide), axis=1) + jnp.sum(
        keyval_term * w_keyval.astype(wide), axis=1
    )
    shard_query = query_term * gain_one
    shard_keyval = keyval_term * gain_one

    grad_query_parts = jnp.stack(
        by_index(
            [grad_query_pre[..., i * q_here : (i + 1) * q_here] for i in range(across)], au_index
        )
    )
    grad_query_parts, grad_keyval_pre = together(grad_query_parts, grad_keyval_pre)
    scaled_one = dot32(grad_keyval_pre, columns[:, q_here:], ((2,), (1,))) + dot32(
        grad_query_parts, query_full, ((0, 3), (0, 2))
    )
    grad_inputs = grad_hidden + inverse_one * (
        scaled_one - unit_one * jnp.mean(scaled_one * unit_one, axis=-1, keepdims=True)
    )
    return (
        result.astype(low),
        grad_inputs.astype(low),
        shard_query,
        shard_keyval,
        shard_out,
        shard_gate,
        shard_up,
        shard_down,
        shard_gain_one,
        shard_gain_two,
    )


def solution(mesh):
    return jax.shard_map(
        on_device,
        mesh=mesh,
        in_specs=(
            P(None, ("row", "au"), None),
            P(),
            P(),
            P(("row", "au"), None),
            P(("row", "au"), None),
            P(("row", "au"), None),
            P(("row", "au"), None),
            P(("row", "au"), None),
            P(("row", "au"), None),
            P(("row", "au")),
            P(("row", "au")),
            P(None, ("row", "au"), None),
            P(None, ("row", "au"), None),
        ),
        out_specs=(
            P(None, ("row", "au"), None),
            P(None, ("row", "au"), None),
            P(("row", "au"), None),
            P(("row", "au"), None),
            P(("row", "au"), None),
            P(("row", "au"), None),
            P(("row", "au"), None),
            P(("row", "au"), None),
            P(("row", "au")),
            P(("row", "au")),
        ),
        check_vma=False,
    )
```

```python
import functools
import math

import jax
import jax.numpy as jnp
from jax import lax
from jax.experimental import pallas as pl
from jax.experimental.pallas import tpu as pltpu
from jax.sharding import PartitionSpec as P

HQ = 16
HEAD_WIDTH = 128
LOG2E = math.log2(math.e)


norm_eps = 1e-05
theta_base = 10000.0


def rotate(values, cosine, sine):
    half = values.shape[-1] // 2
    first = values[..., :half]
    second = values[..., half:]
    return jnp.concatenate(
        [first * cosine - second * sine, second * cosine + first * sine], axis=-1
    )


def rotate_back(grads, cosine, sine):
    half = grads.shape[-1] // 2
    first = grads[..., :half]
    second = grads[..., half:]
    return jnp.concatenate(
        [first * cosine + second * sine, second * cosine - first * sine], axis=-1
    )


def document_info(places, lengths_row):
    starts = jnp.cumsum(lengths_row) - lengths_row
    inside = places[:, None] >= starts[None, :]
    documents = jnp.sum(inside.astype(jnp.int32), axis=1) - 1
    begins = jnp.max(jnp.where(inside, starts[None, :], 0), axis=1)
    return (documents, places - begins)


def angle_table(positions):
    half = HEAD_WIDTH // 2
    inverse_freq = jnp.exp(
        -math.log(theta_base) * (2.0 * jnp.arange(half, dtype=jnp.float32) / HEAD_WIDTH)
    )
    angles = positions.astype(jnp.float32)[..., None] * inverse_freq
    return (jnp.cos(angles), jnp.sin(angles))


low = jnp.bfloat16
wide = jnp.float32


def dot32(left, right, dims):
    return lax.dot_general(left, right, (dims, ((), ())), preferred_element_type=jnp.float32)


NN = ((1,), (0,))
NT = ((1,), (1,))
TN = ((0,), (0,))


def head_columns(ref, heads):
    return jnp.concatenate(
        [ref[:, h * HEAD_WIDTH : (h + 1) * HEAD_WIDTH] for h in range(heads)], axis=0
    )


def visible_bias(places, place, start):
    return jnp.where((places <= place) & (places >= start), 0.0, -1e30)


def attend_kernel(heads, q_ref, kv_ref, own_ref, keys_ref, att_ref, wide_ref, mass_ref, bias_ref):
    count = q_ref.shape[0]
    scale = HEAD_WIDTH**-0.5 * LOG2E

    @pl.when(pl.program_id(1) == 0)
    def _():
        bias_ref[...] = visible_bias(keys_ref[...], own_ref[:, 0:1], own_ref[:, 1:2])

    query = head_columns(q_ref, heads)
    keyval = kv_ref[...]
    scores = dot32(query, keyval[:, :HEAD_WIDTH], NT)
    bias = bias_ref[...]
    for h in range(heads):
        part = scores[h * count : (h + 1) * count] * scale + bias
        highest = jnp.max(part, axis=1, keepdims=True)
        weights = jnp.exp2(part - highest)
        mass = jnp.sum(weights, axis=1, keepdims=True)
        attended = dot32(weights.astype(low), keyval[:, HEAD_WIDTH:], NN) / mass
        columns = slice(h * HEAD_WIDTH, (h + 1) * HEAD_WIDTH)
        att_ref[:, columns] = attended.astype(low)
        wide_ref[:, columns] = attended
        mass_ref[:, columns] = jnp.broadcast_to(highest + jnp.log2(mass), (count, HEAD_WIDTH))


def heads_per_step(slots):
    return max(1, min(4, 4 * 2560 // slots))


def attend(query, keyval, own, keys):
    batches, count, width = query.shape
    slots, kv_width = keyval.shape[1:]
    heads = heads_per_step(slots)
    spec = pl.BlockSpec((None, count, heads * HEAD_WIDTH), lambda b, g: (b, 0, g))
    return pl.pallas_call(
        functools.partial(attend_kernel, heads),
        grid=(batches, HQ // heads),
        in_specs=[
            spec,
            pl.BlockSpec((None, slots, kv_width), lambda b, g: (b, 0, 0)),
            pl.BlockSpec((None, count, 2), lambda b, g: (b, 0, 0)),
            pl.BlockSpec((None, 1, slots), lambda b, g: (b, 0, 0)),
        ],
        out_specs=[spec, spec, spec],
        out_shape=[
            jax.ShapeDtypeStruct(query.shape, low),
            jax.ShapeDtypeStruct(query.shape, wide),
            jax.ShapeDtypeStruct(query.shape, wide),
        ],
        scratch_shapes=[pltpu.VMEM((count, slots), wide)],
        cost_estimate=pl.CostEstimate(
            flops=4 * batches * count * width * slots,
            transcendentals=batches * HQ * count * slots,
            bytes_accessed=16 * batches * count * width,
        ),
        compiler_params=pltpu.CompilerParams(vmem_limit_bytes=48 << 20),
    )(query, keyval, own, keys)


def attend_back_kernel(
    heads,
    chunk,
    q_ref,
    g_ref,
    wide_ref,
    mass_ref,
    kv_ref,
    own_ref,
    keys_ref,
    gq_ref,
    gkv_ref,
    bias_ref,
):
    count = q_ref.shape[0]
    slots = keys_ref.shape[0]
    rate = HEAD_WIDTH**-0.5
    scale = rate * LOG2E

    @pl.when(pl.program_id(1) == 0)
    def _():
        bias_ref[...] = visible_bias(keys_ref[...], own_ref[0:1], own_ref[1:2])
        gkv_ref[...] = jnp.zeros_like(gkv_ref)

    query = head_columns(q_ref, heads)
    grads = head_columns(g_ref, heads)
    mass = head_columns(mass_ref, heads)
    settle = jnp.sum(grads.astype(wide) * head_columns(wide_ref, heads), axis=1, keepdims=True)
    lane = lax.broadcasted_iota(jnp.int32, mass.shape, 1)
    stats = jnp.where(lane == 0, mass, settle).T
    mass_row = stats[0:1]
    settle_row = stats[1:2]
    keyval = kv_ref[...]
    grad_query = jnp.zeros((heads * count, HEAD_WIDTH), wide)
    for c in range(slots // chunk):
        span = slice(c * chunk, (c + 1) * chunk)
        key = keyval[span, :HEAD_WIDTH]
        value = keyval[span, HEAD_WIDTH:]
        weights = jnp.exp2(dot32(key, query, NT) * scale + bias_ref[span, :] - mass_row)
        slope = (weights * (dot32(value, grads, NT) - settle_row)).astype(low)
        gkv_ref[span, HEAD_WIDTH:] += dot32(weights.astype(low), grads, NN)
        gkv_ref[span, :HEAD_WIDTH] += dot32(slope, query, NN) * rate
        grad_query = grad_query + dot32(slope, key, TN)
    for h in range(heads):
        gq_ref[:, h * HEAD_WIDTH : (h + 1) * HEAD_WIDTH] = (
            grad_query[h * count : (h + 1) * count] * rate
        ).astype(low)


def attend_back(query, grads, att_wide, mass, keyval, own, keys, batch):
    batches, count, width = query.shape
    slots, kv_width = keyval.shape[1:]
    heads = heads_per_step(slots)
    own = jnp.tile(own, (1, 1, heads))
    spec = pl.BlockSpec((None, count, heads * HEAD_WIDTH), lambda b, g: (batch, 0, g))
    return pl.pallas_call(
        functools.partial(attend_back_kernel, heads, min(512, slots)),
        grid=(1, HQ // heads),
        in_specs=[
            spec,
            spec,
            spec,
            spec,
            pl.BlockSpec((None, slots, kv_width), lambda b, g: (batch, 0, 0)),
            pl.BlockSpec((None, 2, heads * count), lambda b, g: (batch, 0, 0)),
            pl.BlockSpec((None, slots, 1), lambda b, g: (batch, 0, 0)),
        ],
        out_specs=[
            pl.BlockSpec((None, count, heads * HEAD_WIDTH), lambda b, g: (b, 0, g)),
            pl.BlockSpec((None, slots, kv_width), lambda b, g: (b, 0, 0)),
        ],
        out_shape=[
            jax.ShapeDtypeStruct((1, count, width), low),
            jax.ShapeDtypeStruct((1, slots, kv_width), wide),
        ],
        scratch_shapes=[pltpu.VMEM((slots, heads * count), wide)],
        cost_estimate=pl.CostEstimate(
            flops=10 * count * width * slots,
            transcendentals=HQ * count * slots,
            bytes_accessed=16 * count * width,
        ),
        compiler_params=pltpu.CompilerParams(vmem_limit_bytes=48 << 20),
    )(query, grads, att_wide, mass, keyval, own, keys)


def together(*values):
    return lax.optimization_barrier(values)


def exchange(values, axis, offset):
    members = lax.axis_size(axis)
    return lax.ppermute(values, axis, [(i, i ^ offset) for i in range(members)])


def by_index(parts, place):
    bit = 1
    while bit < len(parts):
        flip = (place & bit) != 0
        parts = [jnp.where(flip, parts[i ^ bit], parts[i]) for i in range(len(parts))]
        bit *= 2
    return parts


def trade_au(parts):
    return [parts[0]] + [exchange(parts[k], "au", k) for k in range(1, len(parts))]


def gather_au(values):
    return trade_au([values] * lax.axis_size("au"))


def bits_of(members):
    return [1 << i for i in range(members.bit_length() - 1)]


def reduce_send(held, bit):
    keys = [k for k in sorted(held) if k & bit]
    return exchange(jnp.stack([held[k] for k in keys]).astype(low), "au", bit)


def reduce_add(held, bit, got):
    keys = [k for k in sorted(held) if k & bit]
    return {
        k ^ bit: held[k ^ bit].astype(wide) + got[i].astype(wide) for i, k in enumerate(keys)
    }


def reduce_au_first(lists):
    bits = bits_of(lax.axis_size("au"))
    return [reduce_send(dict(enumerate(lists[i])), bits[i % len(bits)]) for i in range(2)]


def reduce_au_rest(lists, got):
    bits = bits_of(lax.axis_size("au"))
    done = []
    for i in range(2):
        held = reduce_add(dict(enumerate(lists[i])), bits[i % len(bits)], got[i])
        for j in range(1, len(bits)):
            bit = bits[(i + j) % len(bits)]
            held = reduce_add(held, bit, reduce_send(held, bit))
        done.append(held[0])
    return done


def core_rows(values):
    core = lax.axis_index("row") % 2
    blocks = values.reshape((values.shape[0] // 2, 2) + values.shape[1:])
    return (
        lax.dynamic_index_in_dim(blocks, core, 1, False),
        lax.dynamic_index_in_dim(blocks, 1 - core, 1, False),
    )


def by_core(values):
    rows = lax.axis_size("row")
    blocks = values.reshape(values.shape[:-1] + (rows // 2, 2, values.shape[-1] // rows))
    first = lax.axis_index("row") % 2 == 0
    low_rows, high_rows = blocks[..., 0, :], blocks[..., 1, :]
    flat = values.shape[:-1] + (values.shape[-1] // 2,)
    return (
        jnp.where(first, low_rows, high_rows).reshape(flat),
        jnp.where(first, high_rows, low_rows).reshape(flat),
    )


def reduce_cores(blocks):
    mine, others = core_rows(blocks)
    return mine.astype(wide) + exchange(others.astype(low), "row", 1).astype(wide)


def reduce_chips(here):
    chip = lax.axis_index("row") // 2
    total = lax.dynamic_index_in_dim(here, chip, 0, False)
    here = here.astype(low)
    for k in range(1, here.shape[0]):
        part = lax.dynamic_index_in_dim(here, chip ^ k, 0, False)
        total = total + exchange(part, "row", 2 * k).astype(wide)
    return total


def on_device(
    tokens,
    permutation,
    lengths,
    w_query,
    w_keyval,
    w_out,
    w_gate,
    w_up,
    w_down,
    attn_gain,
    mlp_gain,
    out_grad,
    kv_partner,
):
    batches, local_rows, width = tokens.shape
    across = lax.axis_size("au")
    rows = lax.axis_size("row")
    slot_count = permutation.shape[1]
    q_width = w_query.shape[1]
    kv_width = w_keyval.shape[1]
    own_width = w_query.shape[0]
    ff = w_gate.shape[1]
    ff_here = ff // rows
    ff_own = w_down.shape[0]
    q_here = q_width // across
    row_index = lax.axis_index("row")
    au_index = lax.axis_index("au")
    group_rows = across * local_rows

    gain_one = attn_gain.astype(wide)[:, None]
    gain_two = mlp_gain.astype(wide)[:, None]
    query_scaled = (w_query.astype(wide) * gain_one).astype(low)
    keyval_scaled = (w_keyval.astype(wide) * gain_one).astype(low)
    gate_scaled = (w_gate.astype(wide) * gain_two).astype(low)
    up_scaled = (w_up.astype(wide) * gain_two).astype(low)

    inputs_wide = tokens.astype(wide)
    inverse_one = lax.rsqrt(jnp.mean(inputs_wide * inputs_wide, axis=-1, keepdims=True) + norm_eps)
    unit_one = inputs_wide * inverse_one
    unit_group = jnp.stack(gather_au(unit_one.astype(low)))

    out_rows = lax.all_gather(w_out, "row", axis=0)

    column_blocks = query_scaled.reshape(own_width, across, q_here).transpose(1, 0, 2)
    keyval_blocks = jnp.broadcast_to(keyval_scaled[None], (across, own_width, kv_width))
    column_blocks = lax.all_to_all(
        jnp.concatenate([column_blocks, keyval_blocks], axis=-1), "au", 0, 0
    )
    ff_blocks = jnp.concatenate(
        [gate_scaled.reshape(own_width, rows, ff_here), up_scaled.reshape(own_width, rows, ff_here)],
        axis=-1,
    ).transpose(1, 0, 2)
    column_blocks, unit_group, out_rows, ff_blocks = together(
        column_blocks, unit_group, out_rows, ff_blocks
    )
    column_rows = lax.all_gather(column_blocks, "row", axis=0)
    columns = column_rows.reshape(width, q_here + kv_width)

    au_order = jnp.arange(across, dtype=jnp.int32) ^ au_index
    places = jnp.take(permutation.reshape(batches, rows, across, local_rows), au_order, axis=2)
    key_places = places.reshape(batches, slot_count)
    group_places = lax.dynamic_index_in_dim(places, row_index, 1, False)
    group_positions = jnp.stack(
        [
            document_info(group_places[b].reshape(-1), lengths[b])[1].reshape(across, local_rows)
            for b in range(batches)
        ],
        axis=1,
    )
    group_cosine, group_sine = angle_table(group_positions)
    own = jnp.stack([group_places[:, 0], group_places[:, 0] - group_positions[0]], axis=1)
    cosine = group_cosine[0]
    sine = group_sine[0]

    out_parts = gather_au(core_rows(out_rows)[0])
    columns, ff_blocks, out_parts[1] = together(columns, ff_blocks, out_parts[1])
    ff_rows = lax.all_to_all(ff_blocks, "row", 0, 0)
    projected = dot32(unit_group, columns, ((3,), (0,)))
    key_group = rotate(projected[..., q_here : q_here + HEAD_WIDTH], group_cosine, group_sine)
    keyval = jnp.concatenate([key_group, projected[..., q_here + HEAD_WIDTH :]], axis=-1)
    keyval = keyval.astype(low).transpose(1, 0, 2, 3).reshape(batches, group_rows, kv_width)
    query_group, keyval, w_down, *out_parts = together(
        projected[..., :q_here], keyval, w_down, *out_parts
    )
    down_parts = gather_au(w_down)
    keyval_all = lax.all_gather(keyval, "row", axis=1, tiled=True)
    query_group = query_group.reshape(
        across, batches, local_rows, q_here // HEAD_WIDTH, HEAD_WIDTH
    )
    query_group = rotate(query_group, group_cosine[:, :, :, None], group_sine[:, :, :, None])
    query_group = query_group.astype(low).reshape(across, batches, local_rows, q_here)
    query = jnp.concatenate(by_index(trade_au(list(query_group)), au_index), axis=-1)


    down_full = jnp.zeros((across, ff_own, width), low)
    for k, part in enumerate(down_parts):
        down_full = lax.dynamic_update_index_in_dim(down_full, part, au_index ^ k, 0)
    down_full = down_full.reshape(-1, width)

    key_columns = key_places[:, :, None]
    (
        grads_own,
        keyval_all,
        ff_rows,
        query,
        down_full,
        key_columns,
        *out_parts,
    ) = together(out_grad, keyval_all, ff_rows, query, down_full, key_columns, *out_parts)
    out_half = jnp.zeros((rows // 2, across, own_width, width), low)
    for k, part in enumerate(out_parts):
        out_half = lax.dynamic_update_index_in_dim(out_half, part, au_index ^ k, 1)
    out_half = out_half.reshape(-1, width)
    out_other = exchange(out_half, "row", 1)
    grad_rows = lax.all_gather(grads_own, "row", axis=0).reshape(-1, width)
    ff_parts = gather_au(ff_rows)
    attended, att_wide, log_mass = attend(
        query, keyval_all, own.transpose(0, 2, 1), key_places[:, None, :]
    )
    ff_parts[0] = ff_rows
    attended, ff_parts[1], ff_parts[2] = together(attended, ff_parts[1], ff_parts[2])
    attended_kept = attended
    ff_full = jnp.zeros((rows, across, own_width, 2 * ff_here), low)
    for k, part in enumerate(ff_parts):
        ff_full = lax.dynamic_update_index_in_dim(ff_full, part, au_index ^ k, 1)
    ff_full = ff_full.reshape(width, 2 * ff_here)
    attended_mine, attended_other = by_core(attended)
    hidden = inputs_wide + (
        dot32(attended_mine, out_half, ((2,), (0,))) + dot32(attended_other, out_other, ((2,), (0,)))
    )
    inverse_two = lax.rsqrt(jnp.mean(hidden * hidden, axis=-1, keepdims=True) + norm_eps)
    unit_two = hidden * inverse_two
    unit_low, attended_kept, query_columns = together(
        unit_two.astype(low), attended_kept, core_rows(column_rows[..., :q_here])[0]
    )
    unit_low, grad_rows = together(unit_low, grad_rows)
    unit_rows = lax.all_gather(unit_low, "row", axis=0).reshape(-1, width)
    query_half = gather_au(query_columns)
    pair = lax.dynamic_update_index_in_dim(
        jnp.zeros((rows // 2, 2) + (across * own_width, width), low),
        out_half.reshape(rows // 2, -1, width),
        row_index % 2,
        1,
    )
    out_full = lax.dynamic_update_index_in_dim(
        pair, out_other.reshape(rows // 2, -1, width), 1 - row_index % 2, 1
    ).reshape(q_width, width)
    unit_rows, out_full = together(unit_rows, out_full)

    both = dot32(unit_rows, ff_full, NN)
    gate = both[:, :ff_here]
    up_part = both[:, ff_here:]
    sigmoid_gate = jax.nn.sigmoid(gate)
    inner = (gate * sigmoid_gate * up_part).astype(low)
    grad_inner = dot32(grad_rows, down_full, NT)
    grad_gate = grad_inner * up_part * sigmoid_gate * (1.0 + gate * (1.0 - sigmoid_gate))
    grad_up = grad_inner * gate * sigmoid_gate
    grad_both = jnp.concatenate([grad_gate.astype(low), grad_up.astype(low)], axis=1)
    scaled_two = dot32(grad_both, ff_full, NT).astype(low)
    scaled_two, attended_kept, *query_half = together(scaled_two, attended_kept, *query_half)
    attended_group = jnp.stack(gather_au(attended_kept))
    scaled_two = lax.psum_scatter(
        scaled_two.reshape(rows, batches, local_rows, width), "row"
    ).astype(wide)

    both_term = dot32(unit_rows, grad_both, TN).astype(low)
    both_term = both_term.reshape(rows, across, own_width, 2 * ff_here)
    both_parts = [
        lax.dynamic_index_in_dim(both_term, au_index ^ k, 1, False) for k in range(across)
    ]
    half_rows = own_width // 2
    both_lists = [
        [part[:, i * half_rows : (i + 1) * half_rows] for part in both_parts] for i in range(2)
    ]
    both_first = reduce_au_first(both_lists)
    down_term = dot32(inner, grad_rows, TN).astype(low).reshape(across, ff_own, width)
    down_parts = [
        lax.dynamic_index_in_dim(down_term, au_index ^ k, 0, False) for k in range(across)
    ]
    result_part = dot32(inner, down_full, NN).astype(low)
    result_part = result_part.reshape(rows, batches, local_rows, width)
    query_half = jnp.stack(query_half).reshape(across, rows // 2, -1, q_here)
    query_other = exchange(query_half, "row", 1)
    pair = lax.dynamic_update_index_in_dim(
        jnp.zeros((across, rows // 2, 2) + query_half.shape[2:], low), query_half, row_index % 2, 2
    )
    query_full = lax.dynamic_update_index_in_dim(pair, query_other, 1 - row_index % 2, 2)
    query_full = query_full.reshape(across, width, q_here)
    scaled_two, result_part, down_parts, both_first, query_full, attended_group = together(
        scaled_two, result_part, down_parts, both_first, query_full, attended_group
    )
    both_term = jnp.concatenate(reduce_au_rest(both_lists, both_first), axis=1).astype(low)
    down_parts = trade_au(down_parts)
    result_part = lax.psum_scatter(result_part, "row")

    grad_hidden = out_grad.astype(wide) + inverse_two * (
        scaled_two - unit_two * jnp.mean(scaled_two * unit_two, axis=-1, keepdims=True)
    )
    grad_branch = grad_hidden.astype(low)
    grad_att = dot32(grad_branch, out_full, ((2,), (1,))).astype(low)

    def column_trade(values):
        size = values.shape[-1] // across
        parts = [values[..., i * size : (i + 1) * size] for i in range(across)]
        return jnp.stack(trade_au(by_index(parts, au_index)))

    def owner_columns(part, sizes):
        parts = by_index(trade_au(by_index(list(part), au_index)), au_index)
        ends = [sum(sizes[: i + 1]) for i in range(len(sizes))]
        return [
            jnp.concatenate([p[:, e - n : e] for p in parts], axis=-1).astype(wide)
            for n, e in zip(sizes, ends)
        ]

    group_dims = ((0, 1, 2), (0, 1, 2))
    branch_columns = column_trade(grad_branch)
    grad_query_heads = []
    grad_keyval_term = []
    for b in range(batches):
        grad_query_b, grad_keyval_b = attend_back(
            query, grad_att, att_wide, log_mass, keyval_all, own, key_columns, b
        )
        blocks = grad_keyval_b.reshape(rows, across, local_rows, kv_width)
        mine, others = core_rows(blocks)
        others = exchange(others.astype(low), "row", 1)
        if b == 0:
            grad_query_b, branch_columns, grad_att, both_term = together(
                grad_query_b, branch_columns, grad_att, both_term
            )
            both_term = lax.all_to_all(both_term, "row", 0, 0)
            out_term = dot32(attended_group, branch_columns, group_dims).astype(low)
            grad_att, out_term = together(grad_att, out_term)
            out_term = lax.psum_scatter(out_term.reshape(rows, across, own_width, -1), "row")
        grad_query_heads.append(grad_query_b)
        grad_keyval_term.append(mine + others.astype(wide))
    grad_query_heads = jnp.concatenate(grad_query_heads)
    here = jnp.stack(grad_keyval_term, axis=1)
    grad_query_heads, down_parts[1] = together(grad_query_heads, down_parts[1])

    grad_query_pre = rotate_back(
        grad_query_heads.reshape(batches, local_rows, HQ, HEAD_WIDTH).astype(wide),
        cosine[:, :, None],
        sine[:, :, None],
    )
    grad_query_pre = grad_query_pre.astype(low).reshape(batches, local_rows, q_width)
    query_term = dot32(unit_group, column_trade(grad_query_pre), group_dims).astype(low)
    query_term, result_part = together(query_term, result_part)
    result = hidden + result_part.astype(wide)

    parts = [here[:, :, k] for k in range(across)]
    parts = trade_au([parts[0]] + [part.astype(low) for part in parts[1:]])
    *parts, both_term = together(*parts, both_term)
    grad_keyval_local = reduce_chips(sum(part.astype(wide) for part in parts))
    grad_keyval_local, *down_parts = together(grad_keyval_local, *down_parts)
    grad_keyval_local = (grad_keyval_local + kv_partner.astype(wide)).astype(low)
    grad_key_pre = rotate_back(grad_keyval_local[..., :HEAD_WIDTH].astype(wide), cosine, sine)
    grad_keyval_pre = jnp.concatenate(
        [grad_key_pre, grad_keyval_local[..., HEAD_WIDTH:].astype(wide)], axis=-1
    ).astype(low)
    query_term = lax.psum_scatter(query_term.reshape(rows, across, own_width, -1), "row")
    keyval_term = dot32(unit_one.astype(low), grad_keyval_pre, ((0, 1), (0, 1))).astype(low)
    keyval_term = keyval_term.reshape(rows, across, own_width, kv_width)
    parts = [
        lax.dynamic_index_in_dim(keyval_term, au_index ^ k, 1, False) for k in range(across)
    ]
    keyval_term = sum(part.astype(wide) for part in trade_au(parts))
    keyval_term = reduce_chips(reduce_cores(keyval_term))
    both_term = both_term.astype(wide)
    shard_out, query_term = owner_columns(
        jnp.concatenate([out_term, query_term], axis=-1), [q_here, q_here]
    )

    gate_term = both_term[..., :ff_here].transpose(1, 0, 2).reshape(own_width, ff)
    up_term = both_term[..., ff_here:].transpose(1, 0, 2).reshape(own_width, ff)
    shard_down = sum(part.astype(wide) for part in down_parts)
    shard_gain_two = jnp.sum(
        gate_term * w_gate.astype(wide) + up_term * w_up.astype(wide), axis=1
    )
    shard_gate = gate_term * gain_two
    shard_up = up_term * gain_two
    shard_gain_one = jnp.sum(query_term * w_query.astype(wide), axis=1) + jnp.sum(
        keyval_term * w_keyval.astype(wide), axis=1
    )
    shard_query = query_term * gain_one
    shard_keyval = keyval_term * gain_one

    grad_query_parts = jnp.stack(
        by_index(
            [grad_query_pre[..., i * q_here : (i + 1) * q_here] for i in range(across)], au_index
        )
    )
    grad_query_parts, grad_keyval_pre = together(grad_query_parts, grad_keyval_pre)
    scaled_one = dot32(grad_keyval_pre, columns[:, q_here:], ((2,), (1,))) + dot32(
        grad_query_parts, query_full, ((0, 3), (0, 2))
    )
    grad_inputs = grad_hidden + inverse_one * (
        scaled_one - unit_one * jnp.mean(scaled_one * unit_one, axis=-1, keepdims=True)
    )
    return (
        result.astype(low),
        grad_inputs.astype(low),
        shard_query,
        shard_keyval,
        shard_out,
        shard_gate,
        shard_up,
        shard_down,
        shard_gain_one,
        shard_gain_two,
    )


def solution(mesh):
    return jax.shard_map(
        on_device,
        mesh=mesh,
        in_specs=(
            P(None, ("row", "au"), None),
            P(),
            P(),
            P(("row", "au"), None),
            P(("row", "au"), None),
            P(("row", "au"), None),
            P(("row", "au"), None),
            P(("row", "au"), None),
            P(("row", "au"), None),
            P(("row", "au")),
            P(("row", "au")),
            P(None, ("row", "au"), None),
            P(None, ("row", "au"), None),
        ),
        out_specs=(
            P(None, ("row", "au"), None),
            P(None, ("row", "au"), None),
            P(("row", "au"), None),
            P(("row", "au"), None),
            P(("row", "au"), None),
            P(("row", "au"), None),
            P(("row", "au"), None),
            P(("row", "au"), None),
            P(("row", "au")),
            P(("row", "au")),
        ),
        check_vma=False,
    )
```

```python
import functools
import math

import jax
import jax.numpy as jnp
from jax import lax
from jax.experimental import pallas as pl
from jax.experimental.pallas import tpu as pltpu
from jax.sharding import PartitionSpec as P

HQ = 16
HEAD_WIDTH = 128
LOG2E = math.log2(math.e)


norm_eps = 1e-05
theta_base = 10000.0


def rotate(values, cosine, sine):
    half = values.shape[-1] // 2
    first = values[..., :half]
    second = values[..., half:]
    return jnp.concatenate(
        [first * cosine - second * sine, second * cosine + first * sine], axis=-1
    )


def rotate_back(grads, cosine, sine):
    half = grads.shape[-1] // 2
    first = grads[..., :half]
    second = grads[..., half:]
    return jnp.concatenate(
        [first * cosine + second * sine, second * cosine - first * sine], axis=-1
    )


def document_info(places, lengths_row):
    starts = jnp.cumsum(lengths_row) - lengths_row
    inside = places[:, None] >= starts[None, :]
    documents = jnp.sum(inside.astype(jnp.int32), axis=1) - 1
    begins = jnp.max(jnp.where(inside, starts[None, :], 0), axis=1)
    return (documents, places - begins)


def angle_table(positions):
    half = HEAD_WIDTH // 2
    inverse_freq = jnp.exp(
        -math.log(theta_base) * (2.0 * jnp.arange(half, dtype=jnp.float32) / HEAD_WIDTH)
    )
    angles = positions.astype(jnp.float32)[..., None] * inverse_freq
    return (jnp.cos(angles), jnp.sin(angles))


low = jnp.bfloat16
wide = jnp.float32


def dot32(left, right, dims):
    return lax.dot_general(left, right, (dims, ((), ())), preferred_element_type=jnp.float32)


NN = ((1,), (0,))
NT = ((1,), (1,))
TN = ((0,), (0,))


def head_columns(ref, heads):
    return jnp.concatenate(
        [ref[:, h * HEAD_WIDTH : (h + 1) * HEAD_WIDTH] for h in range(heads)], axis=0
    )


def visible_bias(places, place, start):
    return jnp.where((places <= place) & (places >= start), 0.0, -1e30)


def attend_kernel(heads, q_ref, kv_ref, own_ref, keys_ref, att_ref, wide_ref, mass_ref, bias_ref):
    count = q_ref.shape[0]
    scale = HEAD_WIDTH**-0.5 * LOG2E

    @pl.when(pl.program_id(1) == 0)
    def _():
        bias_ref[...] = visible_bias(keys_ref[...], own_ref[:, 0:1], own_ref[:, 1:2])

    query = head_columns(q_ref, heads)
    keyval = kv_ref[...]
    scores = dot32(query, keyval[:, :HEAD_WIDTH], NT)
    bias = bias_ref[...]
    for h in range(heads):
        part = scores[h * count : (h + 1) * count] * scale + bias
        highest = jnp.max(part, axis=1, keepdims=True)
        weights = jnp.exp2(part - highest)
        mass = jnp.sum(weights, axis=1, keepdims=True)
        attended = dot32(weights.astype(low), keyval[:, HEAD_WIDTH:], NN) / mass
        columns = slice(h * HEAD_WIDTH, (h + 1) * HEAD_WIDTH)
        att_ref[:, columns] = attended.astype(low)
        wide_ref[:, columns] = attended
        mass_ref[:, columns] = jnp.broadcast_to(highest + jnp.log2(mass), (count, HEAD_WIDTH))


def heads_per_step(slots):
    return max(1, min(8, 8 * 2560 // slots))


def attend(query, keyval, own, keys):
    batches, count, width = query.shape
    slots, kv_width = keyval.shape[1:]
    heads = heads_per_step(slots)
    spec = pl.BlockSpec((None, count, heads * HEAD_WIDTH), lambda b, g: (b, 0, g))
    return pl.pallas_call(
        functools.partial(attend_kernel, heads),
        grid=(batches, HQ // heads),
        in_specs=[
            spec,
            pl.BlockSpec((None, slots, kv_width), lambda b, g: (b, 0, 0)),
            pl.BlockSpec((None, count, 2), lambda b, g: (b, 0, 0)),
            pl.BlockSpec((None, 1, slots), lambda b, g: (b, 0, 0)),
        ],
        out_specs=[spec, spec, spec],
        out_shape=[
            jax.ShapeDtypeStruct(query.shape, low),
            jax.ShapeDtypeStruct(query.shape, wide),
            jax.ShapeDtypeStruct(query.shape, wide),
        ],
        scratch_shapes=[pltpu.VMEM((count, slots), wide)],
        cost_estimate=pl.CostEstimate(
            flops=4 * batches * count * width * slots,
            transcendentals=batches * HQ * count * slots,
            bytes_accessed=16 * batches * count * width,
        ),
        compiler_params=pltpu.CompilerParams(vmem_limit_bytes=48 << 20),
    )(query, keyval, own, keys)


def attend_back_kernel(
    heads,
    chunk,
    q_ref,
    g_ref,
    wide_ref,
    mass_ref,
    kv_ref,
    own_ref,
    keys_ref,
    gq_ref,
    gkv_ref,
    bias_ref,
):
    count = q_ref.shape[0]
    slots = keys_ref.shape[0]
    rate = HEAD_WIDTH**-0.5
    scale = rate * LOG2E

    @pl.when(pl.program_id(1) == 0)
    def _():
        bias_ref[...] = visible_bias(keys_ref[...], own_ref[0:1], own_ref[1:2])
        gkv_ref[...] = jnp.zeros_like(gkv_ref)

    query = head_columns(q_ref, heads)
    grads = head_columns(g_ref, heads)
    mass = head_columns(mass_ref, heads)
    settle = jnp.sum(grads.astype(wide) * head_columns(wide_ref, heads), axis=1, keepdims=True)
    lane = lax.broadcasted_iota(jnp.int32, mass.shape, 1)
    stats = jnp.where(lane == 0, mass, settle).T
    mass_row = stats[0:1]
    settle_row = stats[1:2]
    keyval = kv_ref[...]
    grad_query = jnp.zeros((heads * count, HEAD_WIDTH), wide)
    for c in range(slots // chunk):
        span = slice(c * chunk, (c + 1) * chunk)
        key = keyval[span, :HEAD_WIDTH]
        value = keyval[span, HEAD_WIDTH:]
        weights = jnp.exp2(dot32(key, query, NT) * scale + bias_ref[span, :] - mass_row)
        slope = (weights * (dot32(value, grads, NT) - settle_row)).astype(low)
        gkv_ref[span, HEAD_WIDTH:] += dot32(weights.astype(low), grads, NN)
        gkv_ref[span, :HEAD_WIDTH] += dot32(slope, query, NN) * rate
        grad_query = grad_query + dot32(slope, key, TN)
    for h in range(heads):
        gq_ref[:, h * HEAD_WIDTH : (h + 1) * HEAD_WIDTH] = (
            grad_query[h * count : (h + 1) * count] * rate
        ).astype(low)


def attend_back(query, grads, att_wide, mass, keyval, own, keys, batch):
    batches, count, width = query.shape
    slots, kv_width = keyval.shape[1:]
    heads = heads_per_step(slots)
    own = jnp.tile(own, (1, 1, heads))
    spec = pl.BlockSpec((None, count, heads * HEAD_WIDTH), lambda b, g: (batch, 0, g))
    return pl.pallas_call(
        functools.partial(attend_back_kernel, heads, min(512, slots)),
        grid=(1, HQ // heads),
        in_specs=[
            spec,
            spec,
            spec,
            spec,
            pl.BlockSpec((None, slots, kv_width), lambda b, g: (batch, 0, 0)),
            pl.BlockSpec((None, 2, heads * count), lambda b, g: (batch, 0, 0)),
            pl.BlockSpec((None, slots, 1), lambda b, g: (batch, 0, 0)),
        ],
        out_specs=[
            pl.BlockSpec((None, count, heads * HEAD_WIDTH), lambda b, g: (b, 0, g)),
            pl.BlockSpec((None, slots, kv_width), lambda b, g: (b, 0, 0)),
        ],
        out_shape=[
            jax.ShapeDtypeStruct((1, count, width), low),
            jax.ShapeDtypeStruct((1, slots, kv_width), wide),
        ],
        scratch_shapes=[pltpu.VMEM((slots, heads * count), wide)],
        cost_estimate=pl.CostEstimate(
            flops=10 * count * width * slots,
            transcendentals=HQ * count * slots,
            bytes_accessed=16 * count * width,
        ),
        compiler_params=pltpu.CompilerParams(vmem_limit_bytes=48 << 20),
    )(query, grads, att_wide, mass, keyval, own, keys)


def together(*values):
    return lax.optimization_barrier(values)


def exchange(values, axis, offset):
    members = lax.axis_size(axis)
    return lax.ppermute(values, axis, [(i, i ^ offset) for i in range(members)])


def by_index(parts, place):
    bit = 1
    while bit < len(parts):
        flip = (place & bit) != 0
        parts = [jnp.where(flip, parts[i ^ bit], parts[i]) for i in range(len(parts))]
        bit *= 2
    return parts


def trade_au(parts):
    return [parts[0]] + [exchange(parts[k], "au", k) for k in range(1, len(parts))]


def gather_au(values):
    return trade_au([values] * lax.axis_size("au"))


def bits_of(members):
    return [1 << i for i in range(members.bit_length() - 1)]


def reduce_send(held, bit):
    keys = [k for k in sorted(held) if k & bit]
    return exchange(jnp.stack([held[k] for k in keys]).astype(low), "au", bit)


def reduce_add(held, bit, got):
    keys = [k for k in sorted(held) if k & bit]
    return {
        k ^ bit: held[k ^ bit].astype(wide) + got[i].astype(wide) for i, k in enumerate(keys)
    }


def reduce_au_first(lists):
    bits = bits_of(lax.axis_size("au"))
    return [reduce_send(dict(enumerate(lists[i])), bits[i % len(bits)]) for i in range(2)]


def reduce_au_rest(lists, got):
    bits = bits_of(lax.axis_size("au"))
    done = []
    for i in range(2):
        held = reduce_add(dict(enumerate(lists[i])), bits[i % len(bits)], got[i])
        for j in range(1, len(bits)):
            bit = bits[(i + j) % len(bits)]
            held = reduce_add(held, bit, reduce_send(held, bit))
        done.append(held[0])
    return done


def core_rows(values):
    core = lax.axis_index("row") % 2
    blocks = values.reshape((values.shape[0] // 2, 2) + values.shape[1:])
    return (
        lax.dynamic_index_in_dim(blocks, core, 1, False),
        lax.dynamic_index_in_dim(blocks, 1 - core, 1, False),
    )


def by_core(values):
    rows = lax.axis_size("row")
    blocks = values.reshape(values.shape[:-1] + (rows // 2, 2, values.shape[-1] // rows))
    first = lax.axis_index("row") % 2 == 0
    low_rows, high_rows = blocks[..., 0, :], blocks[..., 1, :]
    flat = values.shape[:-1] + (values.shape[-1] // 2,)
    return (
        jnp.where(first, low_rows, high_rows).reshape(flat),
        jnp.where(first, high_rows, low_rows).reshape(flat),
    )


def reduce_cores(blocks):
    mine, others = core_rows(blocks)
    return mine.astype(wide) + exchange(others.astype(low), "row", 1).astype(wide)


def reduce_chips(here):
    chip = lax.axis_index("row") // 2
    total = lax.dynamic_index_in_dim(here, chip, 0, False)
    here = here.astype(low)
    for k in range(1, here.shape[0]):
        part = lax.dynamic_index_in_dim(here, chip ^ k, 0, False)
        total = total + exchange(part, "row", 2 * k).astype(wide)
    return total


def on_device(
    tokens,
    permutation,
    lengths,
    w_query,
    w_keyval,
    w_out,
    w_gate,
    w_up,
    w_down,
    attn_gain,
    mlp_gain,
    out_grad,
    kv_partner,
):
    batches, local_rows, width = tokens.shape
    across = lax.axis_size("au")
    rows = lax.axis_size("row")
    slot_count = permutation.shape[1]
    q_width = w_query.shape[1]
    kv_width = w_keyval.shape[1]
    own_width = w_query.shape[0]
    ff = w_gate.shape[1]
    ff_here = ff // rows
    ff_own = w_down.shape[0]
    q_here = q_width // across
    row_index = lax.axis_index("row")
    au_index = lax.axis_index("au")
    group_rows = across * local_rows

    gain_one = attn_gain.astype(wide)[:, None]
    gain_two = mlp_gain.astype(wide)[:, None]
    query_scaled = (w_query.astype(wide) * gain_one).astype(low)
    keyval_scaled = (w_keyval.astype(wide) * gain_one).astype(low)
    gate_scaled = (w_gate.astype(wide) * gain_two).astype(low)
    up_scaled = (w_up.astype(wide) * gain_two).astype(low)

    inputs_wide = tokens.astype(wide)
    inverse_one = lax.rsqrt(jnp.mean(inputs_wide * inputs_wide, axis=-1, keepdims=True) + norm_eps)
    unit_one = inputs_wide * inverse_one
    unit_group = jnp.stack(gather_au(unit_one.astype(low)))

    out_rows = lax.all_gather(w_out, "row", axis=0)

    column_blocks = query_scaled.reshape(own_width, across, q_here).transpose(1, 0, 2)
    keyval_blocks = jnp.broadcast_to(keyval_scaled[None], (across, own_width, kv_width))
    column_blocks = lax.all_to_all(
        jnp.concatenate([column_blocks, keyval_blocks], axis=-1), "au", 0, 0
    )
    ff_blocks = jnp.concatenate(
        [gate_scaled.reshape(own_width, rows, ff_here), up_scaled.reshape(own_width, rows, ff_here)],
        axis=-1,
    ).transpose(1, 0, 2)
    column_blocks, unit_group, out_rows, ff_blocks = together(
        column_blocks, unit_group, out_rows, ff_blocks
    )
    column_rows = lax.all_gather(column_blocks, "row", axis=0)
    columns = column_rows.reshape(width, q_here + kv_width)

    au_order = jnp.arange(across, dtype=jnp.int32) ^ au_index
    places = jnp.take(permutation.reshape(batches, rows, across, local_rows), au_order, axis=2)
    key_places = places.reshape(batches, slot_count)
    group_places = lax.dynamic_index_in_dim(places, row_index, 1, False)
    group_positions = jnp.stack(
        [
            document_info(group_places[b].reshape(-1), lengths[b])[1].reshape(across, local_rows)
            for b in range(batches)
        ],
        axis=1,
    )
    group_cosine, group_sine = angle_table(group_positions)
    own = jnp.stack([group_places[:, 0], group_places[:, 0] - group_positions[0]], axis=1)
    cosine = group_cosine[0]
    sine = group_sine[0]

    out_parts = gather_au(core_rows(out_rows)[0])
    columns, ff_blocks, out_parts[1] = together(columns, ff_blocks, out_parts[1])
    ff_rows = lax.all_to_all(ff_blocks, "row", 0, 0)
    projected = dot32(unit_group, columns, ((3,), (0,)))
    key_group = rotate(projected[..., q_here : q_here + HEAD_WIDTH], group_cosine, group_sine)
    keyval = jnp.concatenate([key_group, projected[..., q_here + HEAD_WIDTH :]], axis=-1)
    keyval = keyval.astype(low).transpose(1, 0, 2, 3).reshape(batches, group_rows, kv_width)
    query_group, keyval, w_down, *out_parts = together(
        projected[..., :q_here], keyval, w_down, *out_parts
    )
    down_parts = gather_au(w_down)
    keyval_all = lax.all_gather(keyval, "row", axis=1, tiled=True)
    query_group = query_group.reshape(
        across, batches, local_rows, q_here // HEAD_WIDTH, HEAD_WIDTH
    )
    query_group = rotate(query_group, group_cosine[:, :, :, None], group_sine[:, :, :, None])
    query_group = query_group.astype(low).reshape(across, batches, local_rows, q_here)
    query = jnp.concatenate(by_index(trade_au(list(query_group)), au_index), axis=-1)


    down_full = jnp.zeros((across, ff_own, width), low)
    for k, part in enumerate(down_parts):
        down_full = lax.dynamic_update_index_in_dim(down_full, part, au_index ^ k, 0)
    down_full = down_full.reshape(-1, width)

    key_columns = key_places[:, :, None]
    (
        grads_own,
        keyval_all,
        ff_rows,
        query,
        down_full,
        key_columns,
        *out_parts,
    ) = together(out_grad, keyval_all, ff_rows, query, down_full, key_columns, *out_parts)
    out_half = jnp.zeros((rows // 2, across, own_width, width), low)
    for k, part in enumerate(out_parts):
        out_half = lax.dynamic_update_index_in_dim(out_half, part, au_index ^ k, 1)
    out_half = out_half.reshape(-1, width)
    out_other = exchange(out_half, "row", 1)
    grad_rows = lax.all_gather(grads_own, "row", axis=0).reshape(-1, width)
    ff_parts = gather_au(ff_rows)
    attended, att_wide, log_mass = attend(
        query, keyval_all, own.transpose(0, 2, 1), key_places[:, None, :]
    )
    ff_parts[0] = ff_rows
    attended, ff_parts[1], ff_parts[2] = together(attended, ff_parts[1], ff_parts[2])
    attended_kept = attended
    ff_full = jnp.zeros((rows, across, own_width, 2 * ff_here), low)
    for k, part in enumerate(ff_parts):
        ff_full = lax.dynamic_update_index_in_dim(ff_full, part, au_index ^ k, 1)
    ff_full = ff_full.reshape(width, 2 * ff_here)
    attended_mine, attended_other = by_core(attended)
    hidden = inputs_wide + (
        dot32(attended_mine, out_half, ((2,), (0,))) + dot32(attended_other, out_other, ((2,), (0,)))
    )
    inverse_two = lax.rsqrt(jnp.mean(hidden * hidden, axis=-1, keepdims=True) + norm_eps)
    unit_two = hidden * inverse_two
    unit_low, attended_kept, query_columns = together(
        unit_two.astype(low), attended_kept, core_rows(column_rows[..., :q_here])[0]
    )
    unit_low, grad_rows = together(unit_low, grad_rows)
    unit_rows = lax.all_gather(unit_low, "row", axis=0).reshape(-1, width)
    query_half = gather_au(query_columns)
    pair = lax.dynamic_update_index_in_dim(
        jnp.zeros((rows // 2, 2) + (across * own_width, width), low),
        out_half.reshape(rows // 2, -1, width),
        row_index % 2,
        1,
    )
    out_full = lax.dynamic_update_index_in_dim(
        pair, out_other.reshape(rows // 2, -1, width), 1 - row_index % 2, 1
    ).reshape(q_width, width)
    unit_rows, out_full = together(unit_rows, out_full)

    both = dot32(unit_rows, ff_full, NN)
    gate = both[:, :ff_here]
    up_part = both[:, ff_here:]
    sigmoid_gate = jax.nn.sigmoid(gate)
    inner = (gate * sigmoid_gate * up_part).astype(low)
    grad_inner = dot32(grad_rows, down_full, NT)
    grad_gate = grad_inner * up_part * sigmoid_gate * (1.0 + gate * (1.0 - sigmoid_gate))
    grad_up = grad_inner * gate * sigmoid_gate
    grad_both = jnp.concatenate([grad_gate.astype(low), grad_up.astype(low)], axis=1)
    scaled_two = dot32(grad_both, ff_full, NT).astype(low)
    scaled_two, attended_kept, *query_half = together(scaled_two, attended_kept, *query_half)
    attended_group = jnp.stack(gather_au(attended_kept))
    scaled_two = lax.psum_scatter(
        scaled_two.reshape(rows, batches, local_rows, width), "row"
    ).astype(wide)

    both_term = dot32(unit_rows, grad_both, TN).astype(low)
    both_term = both_term.reshape(rows, across, own_width, 2 * ff_here)
    both_parts = [
        lax.dynamic_index_in_dim(both_term, au_index ^ k, 1, False) for k in range(across)
    ]
    half_rows = own_width // 2
    both_lists = [
        [part[:, i * half_rows : (i + 1) * half_rows] for part in both_parts] for i in range(2)
    ]
    both_first = reduce_au_first(both_lists)
    down_term = dot32(inner, grad_rows, TN).astype(low).reshape(across, ff_own, width)
    down_parts = [
        lax.dynamic_index_in_dim(down_term, au_index ^ k, 0, False) for k in range(across)
    ]
    result_part = dot32(inner, down_full, NN).astype(low)
    result_part = result_part.reshape(rows, batches, local_rows, width)
    query_half = jnp.stack(query_half).reshape(across, rows // 2, -1, q_here)
    query_other = exchange(query_half, "row", 1)
    pair = lax.dynamic_update_index_in_dim(
        jnp.zeros((across, rows // 2, 2) + query_half.shape[2:], low), query_half, row_index % 2, 2
    )
    query_full = lax.dynamic_update_index_in_dim(pair, query_other, 1 - row_index % 2, 2)
    query_full = query_full.reshape(across, width, q_here)
    scaled_two, result_part, down_parts, both_first, query_full, attended_group = together(
        scaled_two, result_part, down_parts, both_first, query_full, attended_group
    )
    both_term = jnp.concatenate(reduce_au_rest(both_lists, both_first), axis=1).astype(low)
    down_parts = trade_au(down_parts)
    result_part = lax.psum_scatter(result_part, "row")

    grad_hidden = out_grad.astype(wide) + inverse_two * (
        scaled_two - unit_two * jnp.mean(scaled_two * unit_two, axis=-1, keepdims=True)
    )
    grad_branch = grad_hidden.astype(low)
    grad_att = dot32(grad_branch, out_full, ((2,), (1,))).astype(low)

    def column_trade(values):
        size = values.shape[-1] // across
        parts = [values[..., i * size : (i + 1) * size] for i in range(across)]
        return jnp.stack(trade_au(by_index(parts, au_index)))

    def owner_columns(part, sizes):
        parts = by_index(trade_au(by_index(list(part), au_index)), au_index)
        ends = [sum(sizes[: i + 1]) for i in range(len(sizes))]
        return [
            jnp.concatenate([p[:, e - n : e] for p in parts], axis=-1).astype(wide)
            for n, e in zip(sizes, ends)
        ]

    group_dims = ((0, 1, 2), (0, 1, 2))
    branch_columns = column_trade(grad_branch)
    grad_query_heads = []
    grad_keyval_term = []
    for b in range(batches):
        grad_query_b, grad_keyval_b = attend_back(
            query, grad_att, att_wide, log_mass, keyval_all, own, key_columns, b
        )
        blocks = grad_keyval_b.reshape(rows, across, local_rows, kv_width)
        mine, others = core_rows(blocks)
        others = exchange(others.astype(low), "row", 1)
        if b == 0:
            grad_query_b, branch_columns, grad_att, both_term = together(
                grad_query_b, branch_columns, grad_att, both_term
            )
            both_term = lax.all_to_all(both_term, "row", 0, 0)
            out_term = dot32(attended_group, branch_columns, group_dims).astype(low)
            grad_att, out_term = together(grad_att, out_term)
            out_term = lax.psum_scatter(out_term.reshape(rows, across, own_width, -1), "row")
        grad_query_heads.append(grad_query_b)
        grad_keyval_term.append(mine + others.astype(wide))
    grad_query_heads = jnp.concatenate(grad_query_heads)
    here = jnp.stack(grad_keyval_term, axis=1)
    grad_query_heads, down_parts[1] = together(grad_query_heads, down_parts[1])

    grad_query_pre = rotate_back(
        grad_query_heads.reshape(batches, local_rows, HQ, HEAD_WIDTH).astype(wide),
        cosine[:, :, None],
        sine[:, :, None],
    )
    grad_query_pre = grad_query_pre.astype(low).reshape(batches, local_rows, q_width)
    query_term = dot32(unit_group, column_trade(grad_query_pre), group_dims).astype(low)
    query_term, result_part = together(query_term, result_part)
    result = hidden + result_part.astype(wide)

    parts = [here[:, :, k] for k in range(across)]
    parts = trade_au([parts[0]] + [part.astype(low) for part in parts[1:]])
    *parts, both_term = together(*parts, both_term)
    grad_keyval_local = reduce_chips(sum(part.astype(wide) for part in parts))
    grad_keyval_local, *down_parts = together(grad_keyval_local, *down_parts)
    grad_keyval_local = (grad_keyval_local + kv_partner.astype(wide)).astype(low)
    grad_key_pre = rotate_back(grad_keyval_local[..., :HEAD_WIDTH].astype(wide), cosine, sine)
    grad_keyval_pre = jnp.concatenate(
        [grad_key_pre, grad_keyval_local[..., HEAD_WIDTH:].astype(wide)], axis=-1
    ).astype(low)
    query_term = lax.psum_scatter(query_term.reshape(rows, across, own_width, -1), "row")
    keyval_term = dot32(unit_one.astype(low), grad_keyval_pre, ((0, 1), (0, 1))).astype(low)
    keyval_term = keyval_term.reshape(rows, across, own_width, kv_width)
    parts = [
        lax.dynamic_index_in_dim(keyval_term, au_index ^ k, 1, False) for k in range(across)
    ]
    keyval_term = sum(part.astype(wide) for part in trade_au(parts))
    keyval_term = reduce_chips(reduce_cores(keyval_term))
    both_term = both_term.astype(wide)
    shard_out, query_term = owner_columns(
        jnp.concatenate([out_term, query_term], axis=-1), [q_here, q_here]
    )

    gate_term = both_term[..., :ff_here].transpose(1, 0, 2).reshape(own_width, ff)
    up_term = both_term[..., ff_here:].transpose(1, 0, 2).reshape(own_width, ff)
    shard_down = sum(part.astype(wide) for part in down_parts)
    shard_gain_two = jnp.sum(
        gate_term * w_gate.astype(wide) + up_term * w_up.astype(wide), axis=1
    )
    shard_gate = gate_term * gain_two
    shard_up = up_term * gain_two
    shard_gain_one = jnp.sum(query_term * w_query.astype(wide), axis=1) + jnp.sum(
        keyval_term * w_keyval.astype(wide), axis=1
    )
    shard_query = query_term * gain_one
    shard_keyval = keyval_term * gain_one

    grad_query_parts = jnp.stack(
        by_index(
            [grad_query_pre[..., i * q_here : (i + 1) * q_here] for i in range(across)], au_index
        )
    )
    grad_query_parts, grad_keyval_pre = together(grad_query_parts, grad_keyval_pre)
    scaled_one = dot32(grad_keyval_pre, columns[:, q_here:], ((2,), (1,))) + dot32(
        grad_query_parts, query_full, ((0, 3), (0, 2))
    )
    grad_inputs = grad_hidden + inverse_one * (
        scaled_one - unit_one * jnp.mean(scaled_one * unit_one, axis=-1, keepdims=True)
    )
    return (
        result.astype(low),
        grad_inputs.astype(low),
        shard_query,
        shard_keyval,
        shard_out,
        shard_gate,
        shard_up,
        shard_down,
        shard_gain_one,
        shard_gain_two,
    )


def solution(mesh):
    return jax.shard_map(
        on_device,
        mesh=mesh,
        in_specs=(
            P(None, ("row", "au"), None),
            P(),
            P(),
            P(("row", "au"), None),
            P(("row", "au"), None),
            P(("row", "au"), None),
            P(("row", "au"), None),
            P(("row", "au"), None),
            P(("row", "au"), None),
            P(("row", "au")),
            P(("row", "au")),
            P(None, ("row", "au"), None),
            P(None, ("row", "au"), None),
        ),
        out_specs=(
            P(None, ("row", "au"), None),
            P(None, ("row", "au"), None),
            P(("row", "au"), None),
            P(("row", "au"), None),
            P(("row", "au"), None),
            P(("row", "au"), None),
            P(("row", "au"), None),
            P(("row", "au"), None),
            P(("row", "au")),
            P(("row", "au")),
        ),
        check_vma=False,
    )
```
